128 devices in a mesh: rep: 4 (over z_lo, core), blk: 32 (over y, x, z_hi).
Axes of the slice: x: 4, y: 4, z: 4 (z_hi: 2, z_lo: 2; z = z_hi * 2 + z_lo), core: 2. Of those that a mesh axis runs over, the one named last changes fastest.
Arguments:
- features: bfloat16 [262144, 256], P(('blk', 'rep')), may hold values from -6 to 6
- restriction: float32 [64, 16, 16], replicated, may hold values from -1.5 to 1.5
- mixing: float32 [16, 16], replicated, may hold values from -1.5 to 1.5
- source_index: int32 [32, 4, 2, 2048], P('blk', 'rep'), may hold values from 0 to 8191
- target_index: int32 [32, 4, 2, 2048], P('blk', 'rep'), may hold values from 0 to 8191
- map_index: int32 [32, 4, 2, 2048], P('blk', 'rep'), may hold values from 0 to 63
- edge_counts: int32 [32, 4, 2], P('blk', 'rep'), may hold values from 32 to 2048, as said below
Outputs:
- updated: bfloat16 [262144, 256], P(('blk', 'rep'))
The draws below stay inside these ranges and needn't reach their ends.
Inputs may be any that keep to these rules, and one draw needn't show every extreme that they name: `edge_counts`: each count is max(1, 2048 * l * l // 64) for a whole l from 1 to 8; some tile has exactly 2048 live slots in every draw.
All inputs are finite; a program needn't handle non-finite values.
Results may differ from the reference program's by a relative error of at most 0.0034.
Values may be sent and summed in bfloat16 or wider, within the bound.
A program may use at most 128 MiB of HBM per device.

```python
import jax
import jax.numpy as jnp
from jax import lax

STALK = 16
CHAN = 16
MAPS = 64
CAP = 2048
STEPS = 2
BLOCKS = 32
REPLICAS = 4
BLOCK_NODES = 8192
NODES = 262144


def draw_edge_counts(key, part):
    tile_total = BLOCKS * REPLICAS * STEPS
    levels = jax.random.randint(key, (tile_total,), 1, 9)
    counted = jnp.maximum(1, CAP * levels * levels // 64)
    chosen_tile = jax.random.randint(jax.random.fold_in(key, 7), (), 0, tile_total)
    tile_ids = jnp.arange(tile_total, dtype=jnp.int32)
    counted = jnp.where(tile_ids == chosen_tile, CAP, counted)
    return counted.astype(jnp.int32).reshape(BLOCKS, REPLICAS, STEPS)


def touch_ends(drawn, own_key, low, largest):
    longest = drawn.shape.index(max(drawn.shape))
    spots = []
    for shift in (0, 1):
        where = [jax.random.randint(jax.random.fold_in(own_key, axis), (), 0, length) for axis, length in enumerate(drawn.shape)]
        where[longest] = (where[longest] + shift) % drawn.shape[longest]
        spots.append(tuple(where))
    return drawn.at[spots[0]].set(low).at[spots[1]].set(largest)


def level_of(key, dims, shards, smallest, top_value):
    gain, own = 1.0, jax.random.fold_in(key, 6)
    for axis_at, blocks in shards:
        steps = jnp.exp(jax.random.uniform(jax.random.fold_in(own, axis_at), (blocks,), jnp.float32, smallest / len(shards), top_value / len(shards)))
        gain = gain * jnp.repeat(steps, dims[axis_at] // blocks).reshape([-1 if axis == axis_at else 1 for axis in range(len(dims))])
    return gain


def centred(stream_key, shape, width, limit, split=(), kind=jnp.bfloat16):
    array = jax.random.normal(stream_key, shape, jnp.float32) * width
    if len(split) > 0:
        array = level_of(stream_key, shape, split, -0.22, 0.18) * array
    return jnp.clip(array, min=-limit, max=limit).astype(kind)


def setup_inputs(seed: int = 0) -> dict:
    splits = jax.random.split(jax.random.key(seed), 8)
    return {
        "features": centred(splits[0], (NODES, STALK * CHAN), 1.0, 6.0, ((0, 128),)),
        "restriction": centred(splits[1], (MAPS, STALK, STALK), STALK ** -0.5, 1.5, (), jnp.float32),
        "mixing": centred(splits[2], (CHAN, CHAN), CHAN ** -0.5, 1.5, (), jnp.float32),
        "source_index": touch_ends(jax.random.randint(splits[3], (BLOCKS, REPLICAS, STEPS, CAP), 0, BLOCK_NODES), jax.random.fold_in(splits[3], 1), 0, BLOCK_NODES - 1).astype(jnp.int32),
        "target_index": touch_ends(jax.random.randint(splits[4], (BLOCKS, REPLICAS, STEPS, CAP), 0, BLOCK_NODES), jax.random.fold_in(splits[4], 1), 0, BLOCK_NODES - 1).astype(jnp.int32),
        "map_index": touch_ends(jax.random.randint(splits[5], (BLOCKS, REPLICAS, STEPS, CAP), 0, MAPS), jax.random.fold_in(splits[5], 1), 0, MAPS - 1).astype(jnp.int32),
        "edge_counts": draw_edge_counts(jax.random.fold_in(splits[7], 71), 0),
    }


def reference(features, restriction, mixing, source_index, target_index, map_index, edge_counts):
    feature_width = STALK * CHAN
    tile_total = BLOCKS * REPLICAS * STEPS
    flat_sources = source_index.reshape(tile_total, CAP)
    flat_targets = target_index.reshape(tile_total, CAP)
    flat_maps = map_index.reshape(tile_total, CAP)
    flat_counts = edge_counts.reshape(tile_total)
    tile_ids = jnp.arange(tile_total, dtype=jnp.int32)
    target_blocks = tile_ids // (REPLICAS * STEPS)
    cycle_turns = tile_ids % STEPS
    source_blocks = (target_blocks - cycle_turns) % BLOCKS
    slot_ids = jnp.arange(CAP, dtype=jnp.int32)

    def tile_terms(totals, tile):
        sources, targets, maps, live_count, target_block, source_block = tile
        source_rows = (source_block * BLOCK_NODES + sources).astype(jnp.int32)
        gathered = jnp.take(features, source_rows, axis=0).astype(jnp.float32).reshape(CAP, STALK, CHAN)
        chosen = jnp.take(restriction, maps, axis=0)
        message = jnp.einsum("eij,ejc->eic", chosen, gathered, precision=lax.Precision.HIGHEST)
        message = message.reshape(CAP, feature_width).astype(jnp.bfloat16)
        message = lax.optimization_barrier(message).astype(jnp.float32)
        live = (slot_ids < live_count).astype(jnp.float32)
        target_rows = (target_block * BLOCK_NODES + targets).astype(jnp.int32)
        totals = totals.at[target_rows].add(message * live[:, None])
        return totals, None

    totals = jnp.zeros((NODES, feature_width), jnp.float32)
    totals, _ = lax.scan(tile_terms, totals, (flat_sources, flat_targets, flat_maps, flat_counts, target_blocks, source_blocks))
    mixed = jnp.einsum("nsc,ck->nsk", totals.reshape(NODES, STALK, CHAN), mixing, precision=lax.Precision.HIGHEST)
    updated = features.astype(jnp.float32) + mixed.reshape(NODES, feature_width)
    return updated.astype(jnp.bfloat16)
```

```python
import functools

import jax
import jax.numpy as jnp
from jax import lax
from jax.experimental import pallas as pl
from jax.experimental.pallas import tpu as pltpu
from jax.sharding import PartitionSpec as P

MESH = pl.DeviceIdType.MESH
PIECES = 4
SLOTS = 256
GROUP = 16
ACCS = 2


def exchange_kernel(dims, features, index_ref, restriction_ref, own, prev, list_ref, count_ref, bank_ref,
                    indices, packed, position, index_send, index_recv, send, recv):
    reps, blocks, rows, stalk, channels = dims
    rep = lax.axis_index("rep")
    blk = lax.axis_index("blk")
    pair = lax.rem(rep + 2, 4)
    mate = rep + 1 - 2 * lax.rem(rep, 2)
    far = lax.rem(mate + 2, 4)
    after = lax.rem(blk + 1, blocks)
    before = lax.rem(blk + blocks - 1, blocks)
    to_mate = {"rep": mate, "blk": blk}
    to_pair = {"rep": pair, "blk": blk}
    to_far = {"rep": far, "blk": blk}
    to_next = {"rep": pair, "blk": after}
    from_last = {"rep": pair, "blk": before}

    barrier = pltpu.get_barrier_semaphore()
    for other in (to_mate, to_pair, to_far, to_next, from_last):
        pl.semaphore_signal(barrier, inc=1, device_id=other, device_id_type=MESH)
    pl.semaphore_wait(barrier, 5)

    def index_copy(k, other):
        return pltpu.make_async_remote_copy(
            src_ref=index_ref, dst_ref=indices.at[rep], send_sem=index_send.at[k], recv_sem=index_recv.at[k],
            device_id=other, device_id_type=MESH)

    index_copies = [index_copy(k, other) for k, other in enumerate((to_mate, to_pair, to_far))]
    for copy in index_copies:
        copy.start()

    piece = rows // PIECES

    def rows_of(k):
        return pl.ds(k * piece, piece)

    def remote(family, k, src, dst, other):
        return pltpu.make_async_remote_copy(
            src_ref=src, dst_ref=dst, send_sem=send.at[family, k], recv_sem=recv.at[family, k],
            device_id=other, device_id_type=MESH)

    every = range(PIECES)
    first, second = range(PIECES // 2), range(PIECES // 2, PIECES)
    to_mate_own = [remote(0, k, features.at[rows_of(k), :], own.at[rep, rows_of(k), :], to_mate) for k in every]
    to_pair_own = [remote(1, k, features.at[rows_of(k), :], own.at[rep, rows_of(k), :], to_pair) for k in every]
    to_next_own = [remote(2, k, features.at[rows_of(k), :], prev.at[rep, rows_of(k), :], to_next) for k in every]
    mate_pairs = [remote(3, k, own.at[pair, rows_of(k), :], own.at[pair, rows_of(k), :], to_mate) for k in every]
    mate_lasts = [remote(4, k, prev.at[pair, rows_of(k), :], prev.at[pair, rows_of(k), :], to_mate) for k in every]
    next_pairs = [remote(5, k, own.at[pair, rows_of(k), :], prev.at[pair, rows_of(k), :], to_next) for k in first]
    pair_lasts = [remote(6, k - PIECES // 2, prev.at[pair, rows_of(k), :], prev.at[pair, rows_of(k), :], to_pair) for k in second]
    mate_rest = [remote(7, k, prev.at[rep, rows_of(k), :], prev.at[rep, rows_of(k), :], to_mate) for k in every]

    for k in every:
        to_pair_own[k].start()
        to_next_own[k].start()
        to_mate_own[k].start()

    indices[rep] = index_ref[...]
    for copy in index_copies:
        copy.wait_recv()
    per_rep = index_ref.shape[1]
    chunks = reps * per_rep
    sources = indices[:, 0].reshape(chunks, SLOTS)
    targets = indices[:, 1].reshape(chunks, SLOTS)
    maps = indices[:, 2].reshape(chunks, SLOTS)
    here = (targets // rows) == rep
    earlier = (lax.broadcasted_iota(jnp.int32, (SLOTS, SLOTS), 0) <= lax.broadcasted_iota(jnp.int32, (SLOTS, SLOTS), 1))
    running = jnp.dot(
        here.astype(jnp.float32).astype(jnp.bfloat16), earlier.astype(jnp.float32).astype(jnp.bfloat16),
        preferred_element_type=jnp.float32).astype(jnp.int32)
    count_ref[...] = running[:, SLOTS - 128:]
    position[...] = jnp.where(here, running - 1, -1)
    packed[...] = sources + (targets & (rows - 1)) * 8192 + maps * (8192 * 4096)
    shift = 8 * jnp.minimum(lax.broadcasted_iota(jnp.int32, (8, SLOTS), 0), 3)
    used = lax.broadcasted_iota(jnp.int32, (8, SLOTS), 0) < 4
    place = lax.broadcasted_iota(jnp.int32, (SLOTS, SLOTS), 0)
    slot = lax.broadcasted_iota(jnp.int32, (8, SLOTS), 1)

    def compress(c, carry):
        at = position[pl.ds(c, 1), :]
        word = jnp.broadcast_to(packed[pl.ds(c, 1), :], (8, SLOTS))
        digits = (lax.shift_right_logical(word, shift) & 255).astype(jnp.float32).astype(jnp.bfloat16)
        chosen = jnp.where(place == at, 1.0, 0.0).astype(jnp.bfloat16)
        moved = lax.dot_general(digits, chosen, (((1,), (1,)), ((), ())), preferred_element_type=jnp.float32)
        whole = jnp.where(used, moved.astype(jnp.int32) << shift, 0)
        whole = jnp.sum(whole, axis=0, keepdims=True)
        total = jnp.max(jnp.broadcast_to(at, (8, SLOTS)), axis=1, keepdims=True) + 1
        list_ref[pl.ds(c, 1), :] = jnp.where(slot < total, jnp.broadcast_to(whole, (8, SLOTS)), rows * 8192)[0:1]
        return carry

    lax.fori_loop(0, chunks, compress, 0)

    width = stalk * channels
    bank = restriction_ref[...]
    high = bank.astype(jnp.bfloat16)
    left = bank - high.astype(jnp.float32)
    middle = left.astype(jnp.bfloat16)
    low = (left - middle.astype(jnp.float32)).astype(jnp.bfloat16)
    row_of = lax.broadcasted_iota(jnp.int32, (stalk * stalk, width), 0)
    lane_of = lax.broadcasted_iota(jnp.int32, (stalk * stalk, width), 1) // channels
    for s in range(stalk):
        wanted = lane_of * stalk + ((lane_of - s) & (stalk - 1))
        pick = jnp.where(row_of == wanted, 1.0, 0.0).astype(jnp.bfloat16)
        spread = jnp.dot(high, pick, preferred_element_type=jnp.float32)
        spread = spread + jnp.dot(middle, pick, preferred_element_type=jnp.float32)
        spread = spread + jnp.dot(low, pick, preferred_element_type=jnp.float32)
        bank_ref[:, s, :] = spread

    for k in every:
        to_pair_own[k].wait_recv()
        mate_pairs[k].start()
        if k in first:
            next_pairs[k].start()
        to_next_own[k].wait_recv()
        mate_lasts[k].start()
        if k in second:
            pair_lasts[k - PIECES // 2].start()
    for k in first:
        next_pairs[k].wait_recv()
        mate_rest[k].start()
        pair_lasts[k].wait_recv()
        mate_rest[k + PIECES // 2].start()
    for family in (to_mate_own, mate_pairs, mate_lasts, mate_rest):
        for copy in family:
            copy.wait_recv()
    for copy in index_copies:
        copy.wait_send()
    for family in (to_mate_own, to_pair_own, to_next_own, mate_pairs, mate_lasts, next_pairs, pair_lasts, mate_rest):
        for copy in family:
            copy.wait_send()


def exchange(dims, features, indices, restriction):
    reps, blocks, rows, stalk, channels = dims
    width = stalk * channels
    chunks = reps * indices.shape[1]
    anywhere = pl.BlockSpec(memory_space=pl.ANY)
    vmem = pl.BlockSpec(memory_space=pltpu.VMEM)
    block = jax.ShapeDtypeStruct((reps, rows, width), features.dtype)
    return pl.pallas_call(
        functools.partial(exchange_kernel, dims),
        out_shape=(
            block,
            block,
            jax.ShapeDtypeStruct((chunks, SLOTS), jnp.int32),
            jax.ShapeDtypeStruct((chunks, 128), jnp.int32),
            jax.ShapeDtypeStruct((restriction.shape[0], stalk, width), jnp.float32),
        ),
        in_specs=[anywhere, vmem, vmem],
        out_specs=(anywhere, anywhere, vmem, vmem, vmem),
        scratch_shapes=[
            pltpu.VMEM((reps, *indices.shape), jnp.int32),
            pltpu.VMEM((chunks, SLOTS), jnp.int32),
            pltpu.VMEM((chunks, SLOTS), jnp.int32),
            pltpu.SemaphoreType.DMA((3,)),
            pltpu.SemaphoreType.DMA((3,)),
            pltpu.SemaphoreType.DMA((8, PIECES)),
            pltpu.SemaphoreType.DMA((8, PIECES)),
        ],
        compiler_params=pltpu.CompilerParams(collective_id=0, has_side_effects=True, vmem_limit_bytes=24 << 20),
        name="exchange",
    )(features, indices, restriction)


def column_sums(parts, sub):
    step = 1
    while len(parts) > 1:
        keep = (sub & step) == 0
        half = len(parts) // 2
        joined = []
        for a, b in zip(parts[:half], parts[half:]):
            joined.append(jnp.where(keep, a, b) + pltpu.roll(jnp.where(keep, b, a), step, 0))
        parts = joined
        step *= 2
    return parts[0]


def edge_kernel(dims, feat_ref, own_ref, prev_ref, me_ref, list_ref, count_ref, bank_ref, spread_ref, out_ref,
                stage, table, ring, *rest):
    reps, rows, width, steps, chunks, slots = dims
    accs, (sems,) = rest[:ACCS], rest[ACCS:]
    half = width // 2
    me = me_ref[0]
    def fetch(turn, shard, start):
        dst = stage.at[turn, shard]
        sem = sems.at[turn, shard]
        if turn == 0:
            @pl.when(shard == me)
            def _():
                c = pltpu.make_async_copy(feat_ref, dst, sem)
                c.start() if start else c.wait()
            @pl.when(shard != me)
            def _():
                c = pltpu.make_async_copy(own_ref.at[shard], dst, sem)
                c.start() if start else c.wait()
        else:
            c = pltpu.make_async_copy(prev_ref.at[shard], dst, sem)
            c.start() if start else c.wait()
    for turn in range(steps):
        for shard in range(reps):
            fetch(turn, shard, True)
    def clear(i, _):
        at = pl.ds(pl.multiple_of(i * 128, 128), 128)
        for a in accs:
            a[at, :] = jnp.zeros((128, half), jnp.float32)
        return 0
    lax.fori_loop(0, accs[0].shape[0] // 128, clear, 0)
    lane = lax.broadcasted_iota(jnp.int32, (8, half), 1)
    sub = lax.broadcasted_iota(jnp.int32, (8, half), 0)
    straight = lane >= sub * 16
    for turn in range(steps):
        for shard in range(reps):
            fetch(turn, shard, False)
            def widen(i, _, shard=shard, turn=turn):
                src = pl.ds(pl.multiple_of(i * 128, 128), 128)
                dst = pl.ds(pl.multiple_of(shard * rows + i * 128, 128), 128)
                wide = stage[turn, shard, src, :].astype(jnp.float32)
                table[dst, :] = wide[:, 0:half]
                table[pl.ds(pl.multiple_of((reps + shard) * rows + i * 128, 128), 128), :] = wide[:, half:width]
                return 0
            lax.fori_loop(0, rows // 128, widen, 0)
        def chunk(c, _, turn=turn):
            per = chunks // (reps * steps)
            at = (c // per) * (per * steps) + turn * per + c % per
            n = count_ref[at]
            def group(g, _):
                first = at * slots + g * GROUP
                for base in range(0, GROUP, 8):
                    lows, highs, targets = [], [], []
                    for u in range(8):
                        p = list_ref[first + base + u]
                        src = p & 8191
                        targets.append((p >> 12) & 8190)
                        m = p >> 25
                        a = pltpu.roll(table[pl.ds(src, 8, stride=0), :], 0, 1, stride=16, stride_axis=0)
                        b = pltpu.roll(table[pl.ds(src + reps * rows, 8, stride=0), :], 0, 1, stride=16, stride_axis=0)
                        glo = jnp.where(straight, a, b)
                        ghi = jnp.where(straight, b, a)
                        lows.append(bank_ref[m, 0:8, 0:half] * glo + bank_ref[m, 8:16, 0:half] * ghi)
                        highs.append(bank_ref[m, 0:8, half:width] * ghi + bank_ref[m, 8:16, half:width] * glo)
                    order = (0, 4, 2, 6, 1, 5, 3, 7)
                    for k, parts in enumerate((lows, highs)):
                        message = column_sums([parts[i] for i in order], sub)
                        ring[pl.ds(2 * base + k, 8, stride=2), :] = message.astype(jnp.bfloat16).astype(jnp.float32)
                    for u in range(8):
                        acc = accs[u % ACCS]
                        acc[pl.ds(targets[u], 2), :] += ring[pl.ds(2 * (base + u), 2), :]
                return 0
            lax.fori_loop(0, (n + GROUP - 1) // GROUP, group, 0)
            return 0
        lax.fori_loop(0, chunks // steps, chunk, 0)
    spread = spread_ref[...]
    near = spread.astype(jnp.bfloat16)
    rest_ = (spread - near.astype(jnp.float32)).astype(jnp.bfloat16)
    def finish(i, _):
        at = pl.ds(pl.multiple_of(i * 128, 128), 128)
        sides = []
        for k in range(2):
            where = pl.ds(pl.multiple_of(i * 256, 256) + k, 128, stride=2)
            side = accs[0][where, :]
            for a in accs[1:]:
                side = side + a[where, :]
            sides.append(side)
        total = jnp.concatenate(sides, axis=1)
        top = total.astype(jnp.bfloat16)
        low = (total - top.astype(jnp.float32)).astype(jnp.bfloat16)
        mixed = jnp.dot(top, near, preferred_element_type=jnp.float32)
        mixed = mixed + jnp.dot(low, near, preferred_element_type=jnp.float32)
        mixed = mixed + jnp.dot(top, rest_, preferred_element_type=jnp.float32)
        own = stage[0, me, at, :].astype(jnp.float32)
        out_ref[at, :] = (own + mixed).astype(jnp.bfloat16)
        return 0
    lax.fori_loop(0, rows // 128, finish, 0)


def edges(feat, own, prev, me, lists, counts, bank, spread):
    reps, rows, width = own.shape
    chunks = counts.shape[0]
    slots = lists.shape[0] // chunks
    dims = (reps, rows, width, 2, chunks, slots)
    any_ = pl.BlockSpec(memory_space=pl.ANY)
    smem = pl.BlockSpec(memory_space=pltpu.SMEM)
    vmem = pl.BlockSpec(memory_space=pltpu.VMEM)
    return pl.pallas_call(
        functools.partial(edge_kernel, dims),
        out_shape=jax.ShapeDtypeStruct((rows, width), jnp.bfloat16),
        in_specs=[any_, any_, any_, smem, smem, smem, vmem, vmem],
        out_specs=vmem,
        scratch_shapes=[
            pltpu.VMEM((2, reps, rows, width), jnp.bfloat16),
            pltpu.VMEM((2 * reps * rows, width // 2), jnp.float32),
            pltpu.VMEM((2 * GROUP, width // 2), jnp.float32),
            *[pltpu.VMEM((2 * rows + 128, width // 2), jnp.float32)] * ACCS,
            pltpu.SemaphoreType.DMA((2, reps)),
        ],
        compiler_params=pltpu.CompilerParams(vmem_limit_bytes=60 << 20),
    )(feat, own, prev, me, lists, counts, bank, spread)


def body(features, restriction, mixing, source_index, target_index, map_index, edge_counts):
    rows = features.shape[0]
    stalk = restriction.shape[1]
    channels = mixing.shape[0]
    steps, capacity = source_index.shape[2:]
    dims = (lax.axis_size("rep"), lax.axis_size("blk"), rows, stalk, channels)
    live = lax.broadcasted_iota(jnp.int32, (steps, capacity), 1) < edge_counts[0, 0][:, None]
    targets = jnp.where(live, target_index[0, 0], dims[0] * rows)
    indices = jnp.stack([source_index[0, 0], targets, map_index[0, 0]])
    indices = indices.reshape(3, steps * capacity // SLOTS, SLOTS)
    own, prev, lists, counts, bank = exchange(dims, features, indices, restriction.reshape(-1, stalk * stalk))
    spread = jnp.kron(jnp.eye(stalk, dtype=jnp.float32), mixing)
    me = lax.axis_index("rep").astype(jnp.int32).reshape(1)
    return edges(features, own, prev, me, lists.reshape(-1), counts[:, 127], bank, spread)


def solution(mesh):
    in_specs = (
        P(("blk", "rep"), None),
        P(),
        P(),
        P("blk", "rep", None, None),
        P("blk", "rep", None, None),
        P("blk", "rep", None, None),
        P("blk", "rep", None),
    )
    out_specs = P(("blk", "rep"), None)
    return jax.shard_map(body, mesh=mesh, in_specs=in_specs, out_specs=out_specs, check_vma=False)
```

```python
import functools

import jax
import jax.numpy as jnp
from jax import lax
from jax.experimental import pallas as pl
from jax.experimental.pallas import tpu as pltpu
from jax.sharding import PartitionSpec as P

MESH = pl.DeviceIdType.MESH
PIECES = 4
SLOTS = 256
BLOCK = 8192
GROUP = 16
EIGHTS = GROUP // 8
ACCS = 4


def exchange_kernel(dims, features, source_ref, target_ref, map_ref, count_ref, restriction_ref, mixing_ref,
                    own, prev, list_ref, live_ref, bank_ref, spread_ref,
                    sources, targets, maps, counts, packed, position, home_sem, index_send, index_recv, send, recv):
    reps, blocks, rows, stalk, channels = dims
    width = stalk * channels
    half = width // 2
    rep = lax.axis_index("rep")
    blk = lax.axis_index("blk")
    pair = lax.rem(rep + 2, 4)
    mate = rep + 1 - 2 * lax.rem(rep, 2)
    far = lax.rem(mate + 2, 4)
    after = lax.rem(blk + 1, blocks)
    before = lax.rem(blk + blocks - 1, blocks)
    to_mate = {"rep": mate, "blk": blk}
    to_pair = {"rep": pair, "blk": blk}
    to_far = {"rep": far, "blk": blk}
    to_next = {"rep": pair, "blk": after}
    from_last = {"rep": pair, "blk": before}

    barrier = pltpu.get_barrier_semaphore()
    for other in (to_mate, to_pair, to_far, to_next, from_last):
        pl.semaphore_signal(barrier, inc=1, device_id=other, device_id_type=MESH)
    pl.semaphore_wait(barrier, 5)

    home = pltpu.make_async_copy(features, own.at[rep], home_sem)
    home.start()
    index_copies = []
    for a, (src, dst) in enumerate(((source_ref, sources), (target_ref, targets), (map_ref, maps), (count_ref, counts))):
        for k, other in enumerate((to_mate, to_pair, to_far)):
            index_copies.append(pltpu.make_async_remote_copy(
                src_ref=src, dst_ref=dst.at[rep], send_sem=index_send.at[a, k], recv_sem=index_recv.at[a, k],
                device_id=other, device_id_type=MESH))
    for copy in index_copies:
        copy.start()

    piece = rows // PIECES

    def rows_of(k):
        return pl.ds(k * piece, piece)

    def remote(family, k, src, dst, other):
        return pltpu.make_async_remote_copy(
            src_ref=src, dst_ref=dst, send_sem=send.at[family, k], recv_sem=recv.at[family, k],
            device_id=other, device_id_type=MESH)

    every = range(PIECES)
    first, second = range(PIECES // 2), range(PIECES // 2, PIECES)
    to_mate_own = [remote(0, k, features.at[rows_of(k), :], own.at[rep, rows_of(k), :], to_mate) for k in every]
    to_pair_own = [remote(1, k, features.at[rows_of(k), :], own.at[rep, rows_of(k), :], to_pair) for k in every]
    to_next_own = [remote(2, k, features.at[rows_of(k), :], prev.at[rep, rows_of(k), :], to_next) for k in every]
    mate_pairs = [remote(3, k, own.at[pair, rows_of(k), :], own.at[pair, rows_of(k), :], to_mate) for k in every]
    mate_lasts = [remote(4, k, prev.at[pair, rows_of(k), :], prev.at[pair, rows_of(k), :], to_mate) for k in every]
    next_pairs = [remote(5, k, own.at[pair, rows_of(k), :], prev.at[pair, rows_of(k), :], to_next) for k in first]
    pair_lasts = [remote(6, k - PIECES // 2, prev.at[pair, rows_of(k), :], prev.at[pair, rows_of(k), :], to_pair) for k in second]
    mate_rest = [remote(7, k, prev.at[rep, rows_of(k), :], prev.at[rep, rows_of(k), :], to_mate) for k in every]

    for k in every:
        to_pair_own[k].start()
        to_next_own[k].start()
        to_mate_own[k].start()

    for src, dst in ((source_ref, sources), (target_ref, targets), (map_ref, maps), (count_ref, counts)):
        dst[rep] = src[...]
    for copy in index_copies:
        copy.wait_recv()
    steps, capacity = source_ref.shape[2:]
    runs = capacity // SLOTS
    chunks = reps * runs * steps
    spot = lax.broadcasted_iota(jnp.int32, (steps, SLOTS), 1)
    for r in range(reps):
        live = counts[r, 0]
        live = jnp.concatenate([jnp.broadcast_to(live[:, s:s + 1], (1, SLOTS)) for s in range(steps)], axis=0)
        for j in range(runs):
            part = pl.ds(j * SLOTS, SLOTS)
            to = sources.at[r, 0, 0, :, part][...]
            hit = targets.at[r, 0, 0, :, part][...]
            by = maps.at[r, 0, 0, :, part][...]
            here = (hit // rows == rep) & (spot + j * SLOTS < live)
            at = pl.ds((r * runs + j) * steps, steps)
            packed[at, :] = to + by * BLOCK + (hit & (rows - 1)) * (BLOCK * 128)
            position[at, :] = jnp.where(here, 1, 0)
    earlier = (lax.broadcasted_iota(jnp.int32, (SLOTS, SLOTS), 0) <= lax.broadcasted_iota(jnp.int32, (SLOTS, SLOTS), 1))
    here = position[...]
    running = jnp.dot(
        here.astype(jnp.float32).astype(jnp.bfloat16), earlier.astype(jnp.float32).astype(jnp.bfloat16),
        preferred_element_type=jnp.float32).astype(jnp.int32)
    live_ref[...] = running[:, SLOTS - 128:]
    position[...] = jnp.where(here > 0, running - 1, -1)
    unused = rows * (BLOCK * 128) - 2**32
    shift = 8 * jnp.minimum(lax.broadcasted_iota(jnp.int32, (8, SLOTS), 0), 3)
    used = lax.broadcasted_iota(jnp.int32, (8, SLOTS), 0) < 4
    place = lax.broadcasted_iota(jnp.int32, (SLOTS, SLOTS), 0)
    slot = lax.broadcasted_iota(jnp.int32, (8, SLOTS), 1)
    list_ref[chunks:chunks + 8, :] = jnp.full((8, SLOTS), unused, jnp.int32)

    def compress(c, carry):
        at = position[pl.ds(c, 1), :]
        word = jnp.broadcast_to(packed[pl.ds(c, 1), :], (8, SLOTS))
        digits = (lax.shift_right_logical(word, shift) & 255).astype(jnp.float32).astype(jnp.bfloat16)
        chosen = jnp.where(place == at, 1.0, 0.0).astype(jnp.bfloat16)
        moved = lax.dot_general(digits, chosen, (((1,), (1,)), ((), ())), preferred_element_type=jnp.float32)
        whole = jnp.where(used, moved.astype(jnp.int32) << shift, 0)
        whole = jnp.sum(whole, axis=0, keepdims=True)
        total = jnp.max(jnp.broadcast_to(at, (8, SLOTS)), axis=1, keepdims=True) + 1
        list_ref[pl.ds(c, 1), :] = jnp.where(slot < total, jnp.broadcast_to(whole, (8, SLOTS)), unused)[0:1]
        return carry

    lax.fori_loop(0, chunks, compress, 0)

    count = restriction_ref.shape[0]
    flat = restriction_ref[...].reshape(count * stalk, stalk)

    def three(x):
        high = x.astype(jnp.bfloat16)
        left = x - high.astype(jnp.float32)
        middle = left.astype(jnp.bfloat16)
        return high, middle, (left - middle.astype(jnp.float32)).astype(jnp.bfloat16)

    def ones(shape, test):
        return jnp.where(
            test(lax.broadcasted_iota(jnp.int32, shape, 0), lax.broadcasted_iota(jnp.int32, shape, 1)), 1.0, 0.0
        ).astype(jnp.bfloat16)

    eye = ones((stalk, stalk), lambda p, q: p == q)
    same = ones((width, width), lambda p, q: p // stalk == q // stalk)
    wide = ones((width, width), lambda p, q: (p & (stalk - 1)) == q // channels)
    flipped = [
        lax.dot_general(eye, part, (((1,), (1,)), ((), ())), preferred_element_type=jnp.float32).astype(jnp.bfloat16)
        for part in three(flat)]
    per = width // stalk
    for q in range(count // per):
        total = jnp.zeros((width, width), jnp.float32)
        for part in flipped:
            stacked = jnp.concatenate([part[:, q * width:(q + 1) * width]] * per, axis=0) * same
            total = total + jnp.dot(stacked, wide, preferred_element_type=jnp.float32)
        for m in range(per):
            for h in range(2):
                for l in range(2):
                    bank_ref[pl.ds(((q * per + m) * 4 + 2 * h + l) * 8, 8), :] = total[
                        m * stalk + 8 * h:m * stalk + 8 * h + 8, l * half:(l + 1) * half]

    tall = ones((width, channels), lambda p, q: (p & (channels - 1)) == q)
    broad = ones((channels, width), lambda p, q: p == (q & (channels - 1)))
    blocked = ones((width, width), lambda p, q: p // channels == q // channels)
    for k, part in enumerate(three(mixing_ref[...])[:2]):
        part = jnp.dot(tall, part, preferred_element_type=jnp.float32).astype(jnp.bfloat16)
        spread_ref[k] = jnp.dot(part, broad, preferred_element_type=jnp.float32).astype(jnp.bfloat16) * blocked

    for k in every:
        to_pair_own[k].wait_recv()
        mate_pairs[k].start()
        if k in first:
            next_pairs[k].start()
        to_next_own[k].wait_recv()
        mate_lasts[k].start()
        if k in second:
            pair_lasts[k - PIECES // 2].start()
    for k in first:
        next_pairs[k].wait_recv()
        mate_rest[k].start()
        pair_lasts[k].wait_recv()
        mate_rest[k + PIECES // 2].start()
    for family in (to_mate_own, mate_pairs, mate_lasts, mate_rest):
        for copy in family:
            copy.wait_recv()
    home.wait()
    for copy in index_copies:
        copy.wait_send()
    for family in (to_mate_own, to_pair_own, to_next_own, mate_pairs, mate_lasts, next_pairs, pair_lasts, mate_rest):
        for copy in family:
            copy.wait_send()


def exchange(dims, features, sources, targets, maps, counts, restriction, mixing):
    reps, blocks, rows, stalk, channels = dims
    width = stalk * channels
    chunks = reps * sources.size // SLOTS
    vmem = pl.BlockSpec(memory_space=pltpu.VMEM)
    block = jax.ShapeDtypeStruct((reps, rows, width), features.dtype)
    return pl.pallas_call(
        functools.partial(exchange_kernel, dims),
        out_shape=(
            block,
            block,
            jax.ShapeDtypeStruct((chunks + 8, SLOTS), jnp.int32),
            jax.ShapeDtypeStruct((chunks, 128), jnp.int32),
            jax.ShapeDtypeStruct((2 * restriction.shape[0] * stalk, width // 2), jnp.float32),
            jax.ShapeDtypeStruct((2, width, width), jnp.bfloat16),
        ),
        in_specs=[pl.BlockSpec(memory_space=pl.ANY)] + [vmem] * 6,
        out_specs=(vmem,) * 6,
        scratch_shapes=[
            pltpu.VMEM((reps, *sources.shape), jnp.int32),
            pltpu.VMEM((reps, *sources.shape), jnp.int32),
            pltpu.VMEM((reps, *sources.shape), jnp.int32),
            pltpu.VMEM((reps, *counts.shape), jnp.int32),
            pltpu.VMEM((chunks, SLOTS), jnp.int32),
            pltpu.VMEM((chunks, SLOTS), jnp.int32),
            pltpu.SemaphoreType.DMA,
            pltpu.SemaphoreType.DMA((4, 3)),
            pltpu.SemaphoreType.DMA((4, 3)),
            pltpu.SemaphoreType.DMA((8, PIECES)),
            pltpu.SemaphoreType.DMA((8, PIECES)),
        ],
        compiler_params=pltpu.CompilerParams(collective_id=0, has_side_effects=True, vmem_limit_bytes=28 << 20),
        name="exchange",
    )(features, sources, targets, maps, counts, restriction, mixing)


def column_sums(parts, sub):
    step = 1
    while len(parts) > 1:
        keep = (sub & step) == 0
        half = len(parts) // 2
        joined = []
        for a, b in zip(parts[:half], parts[half:]):
            joined.append(jnp.where(keep, a, b) + pltpu.roll(jnp.where(keep, b, a), step, 0))
        parts = joined
        step *= 2
    return parts[0]


def edge_kernel(dims, own_ref, prev_ref, list_ref, count_ref, bank_ref, spread_ref, out_ref,
                table, ring_even, ring_odd, starts, *rest):
    reps, rows, width, steps, chunks, slots = dims
    accs = rest
    half = width // 2
    rings = (ring_even, ring_odd)
    me = lax.axis_index("rep")
    def clear(i, _):
        at = pl.ds(pl.multiple_of(i * 128, 128), 128)
        for a in accs:
            a[at, :] = jnp.zeros((128, half), jnp.float32)
        return 0
    lax.fori_loop(0, accs[0].shape[0] // 128, clear, 0)
    sub = lax.broadcasted_iota(jnp.int32, (8, half), 0)
    diagonal = jnp.where(
        lax.broadcasted_iota(jnp.int32, (16, half), 1) // 16 == (lax.broadcasted_iota(jnp.int32, (16, half), 0) & 7), 1.0, 0.0
    ).astype(jnp.bfloat16)
    k_at = lax.broadcasted_iota(jnp.int32, (width, width), 0)
    n_at = lax.broadcasted_iota(jnp.int32, (width, width), 1)
    repeat = jnp.where((k_at % 16 == n_at % 16) & (k_at // half == n_at // half), 1.0, 0.0).astype(jnp.bfloat16)
    for turn in range(steps):
        for shard in range(reps):
            def widen(i, _, shard=shard, turn=turn):
                src = pl.ds(pl.multiple_of(i * 128, 128), 128)
                dst = pl.ds(pl.multiple_of(shard * rows + i * 128, 128), 128)
                wide = (own_ref, prev_ref)[turn][shard, src, :].astype(jnp.float32)
                table[dst, :] = wide[:, 0:half]
                table[pl.ds(pl.multiple_of((reps + shard) * rows + i * 128, 128), 128), :] = wide[:, half:width]
                return 0
            lax.fori_loop(0, rows // 128, widen, 0)
        per = chunks // (reps * steps)

        def plan(c, filled, turn=turn):
            at = c * steps + turn
            eights = (count_ref[at, 127] + 7) // 8

            def note(k, carry):
                starts[filled + k] = at * slots + 8 * k
                return carry

            lax.fori_loop(0, eights, note, 0)
            return filled + eights

        eights = lax.fori_loop(0, chunks // steps, plan, 0)
        for k in range(2 * EIGHTS):
            starts[eights + k] = chunks * slots
        groups = (eights + 2 * EIGHTS - 1) // (2 * EIGHTS)
        for k in range(2 * EIGHTS):
            starts[2 * EIGHTS * groups + k] = chunks * slots

        def words(g):
            found = []
            for k in range(EIGHTS):
                first = starts[g * EIGHTS + k]
                found += [list_ref[first + u] for u in range(8)]
            return found

        def load(now, sides, staged=None):
            for side in range(2):
                tiles = []
                for word in now[side * GROUP // 2:(side + 1) * GROUP // 2]:
                    src = word & 8191
                    both = jnp.concatenate(
                        [table[pl.ds(src, 8, stride=0), :], table[pl.ds(src + reps * rows, 8, stride=0), :]], axis=0)
                    tiles.append(both.astype(jnp.bfloat16) * diagonal)
                pairs = [jnp.concatenate(tiles[u:u + 2], axis=1) for u in range(0, GROUP // 2, 2)]
                pltpu.matmul_acc_lhs(sides[side], jnp.concatenate(pairs, axis=0), load_staged_rhs=staged)

        def add_up(now, popped, ring):
            for side in range(2):
                repeated = popped[side]
                for base in range(side * GROUP // 2, (side + 1) * GROUP // 2, 8):
                    lows, highs = [], []
                    for u in range(base, base + 8):
                        maps = bank_ref[pl.ds(pl.multiple_of((now[u] >> 8) & 2016, 32), 32), :]
                        row = u % (GROUP // 2) // 2 * 16
                        lane = u % 2 * half
                        top = repeated[row:row + 8, lane:lane + half]
                        low = repeated[row + 8:row + 16, lane:lane + half]
                        lows.append(maps[0:8] * top + maps[16:24] * low)
                        highs.append(maps[8:16] * top + maps[24:32] * low)
                    for k, parts in enumerate((lows, highs)):
                        message = column_sums([parts[i] for i in (0, 4, 2, 6, 1, 5, 3, 7)], sub)
                        ring[pl.ds(2 * base + k, 8, stride=2), :] = message.astype(jnp.bfloat16).astype(jnp.float32)
            for u in range(GROUP):
                acc = accs[u % ACCS]
                acc[pl.ds(lax.shift_right_logical(now[u], 19), 2), :] += ring[pl.ds(2 * u, 2), :]

        def run(*sides):
            even, odd = sides[:2], sides[2:]
            for side in range(2):
                pltpu.matmul_push_rhs(repeat, 0, side)
            load(words(0), even, 0)
            load(words(1), odd)

            def group(g, carry):
                for which, sides in enumerate((even, odd)):
                    popped = [pltpu.matmul_pop(side) for side in sides]
                    load(words(2 * g + which + 2), sides)
                    add_up(words(2 * g + which), popped, rings[which])
                return carry

            lax.fori_loop(0, groups, group, 0)
            for side in (*even, *odd):
                rings[0][0:8, :] = pltpu.matmul_pop(side)[0:8, 0:half]

        pl.run_scoped(run, *[pltpu.ACC(side)((4 * GROUP, width), jnp.float32) for side in (0, 1, 0, 1)])
    block = 128

    def finish(sides, i, carry):
        at = pl.ds(pl.multiple_of(i * block, block), block)
        halves = []
        for k in range(2):
            where = pl.ds(pl.multiple_of(i * 2 * block, 2 * block) + k, block, stride=2)
            side = accs[0][where, :]
            for a in accs[1:]:
                side = side + a[where, :]
            halves.append(side)
        total = jnp.concatenate(halves, axis=1)
        top = total.astype(jnp.bfloat16)
        low = (total - top.astype(jnp.float32)).astype(jnp.bfloat16)
        pltpu.matmul_acc_lhs(sides[0], top)
        pltpu.matmul_acc_lhs(sides[1], top)
        pltpu.matmul_acc_lhs(sides[0], low)
        mixed = pltpu.matmul_pop(sides[0]) + pltpu.matmul_pop(sides[1])
        own = own_ref[me, at, :].astype(jnp.float32)
        out_ref[at, :] = (own + mixed).astype(jnp.bfloat16)
        return carry

    def mix(*sides):
        blank = jnp.zeros((block, width), jnp.bfloat16)
        for side, weights in enumerate((spread_ref[0], spread_ref[1])):
            pltpu.matmul_push_rhs(weights, 0, side)
            pltpu.matmul_acc_lhs(sides[side], blank, load_staged_rhs=0)
        lax.fori_loop(0, rows // block, functools.partial(finish, sides), 0)

    pl.run_scoped(mix, *[pltpu.ACC(side)((block, width), jnp.float32) for side in range(2)])


def edges(own, prev, lists, counts, bank, spread):
    reps, rows, width = own.shape
    chunks = counts.shape[0]
    dims = (reps, rows, width, 2, chunks, SLOTS)
    smem = pl.BlockSpec(memory_space=pltpu.SMEM)
    vmem = pl.BlockSpec(memory_space=pltpu.VMEM)
    return pl.pallas_call(
        functools.partial(edge_kernel, dims),
        out_shape=jax.ShapeDtypeStruct((rows, width), own.dtype),
        in_specs=[vmem, vmem, smem, smem, vmem, vmem],
        out_specs=vmem,
        scratch_shapes=[
            pltpu.VMEM((2 * reps * rows, width // 2), jnp.float32),
            pltpu.VMEM((2 * GROUP, width // 2), jnp.float32),
            pltpu.VMEM((2 * GROUP, width // 2), jnp.float32),
            pltpu.SMEM((lists.shape[0] // 8 + 16,), jnp.int32),
            *[pltpu.VMEM((2 * rows + 128, width // 2), jnp.float32)] * ACCS,
        ],
        compiler_params=pltpu.CompilerParams(vmem_limit_bytes=36 << 20),
        name="edges",
    )(own, prev, lists, counts, bank, spread)


def body(features, restriction, mixing, source_index, target_index, map_index, edge_counts):
    rows = features.shape[0]
    stalk = restriction.shape[1]
    channels = mixing.shape[0]
    dims = (lax.axis_size("rep"), lax.axis_size("blk"), rows, stalk, channels)
    own, prev, lists, counts, bank, spread = exchange(
        dims, features, source_index, target_index, map_index, edge_counts, restriction, mixing)
    return edges(own, prev, lists.reshape(-1), counts, bank, spread)


def solution(mesh):
    in_specs = (
        P(("blk", "rep"), None),
        P(),
        P(),
        P("blk", "rep", None, None),
        P("blk", "rep", None, None),
        P("blk", "rep", None, None),
        P("blk", "rep", None),
    )
    out_specs = P(("blk", "rep"), None)
    step = jax.shard_map(body, mesh=mesh, in_specs=in_specs, out_specs=out_specs, check_vma=False)

    def run(*args):
        with jax.sharding.use_abstract_mesh(mesh.abstract_mesh):
            return step(*args)

    return run
```

```python
import functools

import jax
import jax.numpy as jnp
from jax import lax
from jax.experimental import pallas as pl
from jax.experimental.pallas import tpu as pltpu
from jax.sharding import PartitionSpec as P

MESH = pl.DeviceIdType.MESH
PIECES = 4
SLOTS = 256
BLOCK = 8192
GROUP = 16
EIGHTS = GROUP // 8
ACCS = 4


def exchange_kernel(dims, features, source_ref, target_ref, map_ref, count_ref, restriction_ref, mixing_ref,
                    own, prev, near_table, far_table, list_ref, live_ref, bank_ref, spread_ref,
                    sources, targets, maps, counts, restrictions, mixings, packed, position,
                    home_sem, index_send, index_recv, send, recv):
    reps, blocks, rows, stalk, channels = dims
    width = stalk * channels
    half = width // 2
    rep = lax.axis_index("rep")
    blk = lax.axis_index("blk")
    pair = lax.rem(rep + 2, 4)
    mate = rep + 1 - 2 * lax.rem(rep, 2)
    far = lax.rem(mate + 2, 4)
    after = lax.rem(blk + 1, blocks)
    before = lax.rem(blk + blocks - 1, blocks)
    to_mate = {"rep": mate, "blk": blk}
    to_pair = {"rep": pair, "blk": blk}
    to_far = {"rep": far, "blk": blk}
    to_next = {"rep": pair, "blk": after}
    from_last = {"rep": pair, "blk": before}

    home = [pltpu.make_async_copy(src, dst, home_sem.at[k]) for k, (src, dst) in enumerate((
        (source_ref, sources.at[rep]), (target_ref, targets.at[rep]), (map_ref, maps.at[rep]), (count_ref, counts.at[rep]),
        (features, own.at[rep]), (restriction_ref, restrictions), (mixing_ref, mixings)))]
    for copy in home:
        copy.start()

    barrier = pltpu.get_barrier_semaphore()
    for other in (to_mate, to_pair, to_far, to_next, from_last):
        pl.semaphore_signal(barrier, inc=1, device_id=other, device_id_type=MESH)
    pl.semaphore_wait(barrier, 5)

    index_copies = []
    for a, (src, dst) in enumerate(((source_ref, sources), (target_ref, targets), (map_ref, maps), (count_ref, counts))):
        for k, other in enumerate((to_mate, to_pair, to_far)):
            index_copies.append(pltpu.make_async_remote_copy(
                src_ref=src, dst_ref=dst.at[rep], send_sem=index_send.at[a, k], recv_sem=index_recv.at[a, k],
                device_id=other, device_id_type=MESH))
    for copy in index_copies:
        copy.start()

    piece = rows // PIECES

    def rows_of(k):
        return pl.ds(k * piece, piece)

    def remote(family, k, src, dst, other):
        return pltpu.make_async_remote_copy(
            src_ref=src, dst_ref=dst, send_sem=send.at[family, k], recv_sem=recv.at[family, k],
            device_id=other, device_id_type=MESH)

    every = range(PIECES)
    first, second = range(PIECES // 2), range(PIECES // 2, PIECES)
    to_mate_own = [remote(0, k, features.at[rows_of(k), :], own.at[rep, rows_of(k), :], to_mate) for k in every]
    to_pair_own = [remote(1, k, features.at[rows_of(k), :], own.at[rep, rows_of(k), :], to_pair) for k in every]
    to_next_own = [remote(2, k, features.at[rows_of(k), :], prev.at[rep, rows_of(k), :], to_next) for k in every]
    mate_pairs = [remote(3, k, own.at[pair, rows_of(k), :], own.at[pair, rows_of(k), :], to_mate) for k in every]
    mate_lasts = [remote(4, k, prev.at[pair, rows_of(k), :], prev.at[pair, rows_of(k), :], to_mate) for k in every]
    next_pairs = [remote(5, k, own.at[pair, rows_of(k), :], prev.at[pair, rows_of(k), :], to_next) for k in first]
    pair_lasts = [remote(6, k - PIECES // 2, prev.at[pair, rows_of(k), :], prev.at[pair, rows_of(k), :], to_pair) for k in second]
    mate_rest = [remote(7, k, prev.at[rep, rows_of(k), :], prev.at[rep, rows_of(k), :], to_mate) for k in every]

    for k in every:
        to_pair_own[k].start()
        to_next_own[k].start()
        to_mate_own[k].start()

    for copy in home:
        copy.wait()
    for copy in index_copies:
        copy.wait_recv()
    steps, capacity = source_ref.shape[2:]
    runs = capacity // SLOTS
    chunks = reps * runs * steps
    spot = lax.broadcasted_iota(jnp.int32, (steps, SLOTS), 1)
    for r in range(reps):
        live = counts[r, 0]
        live = jnp.concatenate([jnp.broadcast_to(live[:, s:s + 1], (1, SLOTS)) for s in range(steps)], axis=0)
        for j in range(runs):
            part = pl.ds(j * SLOTS, SLOTS)
            to = sources.at[r, 0, 0, :, part][...]
            hit = targets.at[r, 0, 0, :, part][...]
            by = maps.at[r, 0, 0, :, part][...]
            here = (hit // rows == rep) & (spot + j * SLOTS < live)
            at = pl.ds((r * runs + j) * steps, steps)
            packed[at, :] = to + by * BLOCK + (hit & (rows - 1)) * (BLOCK * 128)
            position[at, :] = jnp.where(here, 1, 0)
    earlier = (lax.broadcasted_iota(jnp.int32, (SLOTS, SLOTS), 0) <= lax.broadcasted_iota(jnp.int32, (SLOTS, SLOTS), 1))
    here = position[...]
    running = jnp.dot(
        here.astype(jnp.float32).astype(jnp.bfloat16), earlier.astype(jnp.float32).astype(jnp.bfloat16),
        preferred_element_type=jnp.float32).astype(jnp.int32)
    live_ref[...] = running[:, SLOTS - 128:]
    position[...] = jnp.where(here > 0, running - 1, -1)
    unused = rows * (BLOCK * 128) - 2**32
    shift = 8 * jnp.minimum(lax.broadcasted_iota(jnp.int32, (8, SLOTS), 0), 3)
    used = lax.broadcasted_iota(jnp.int32, (8, SLOTS), 0) < 4
    place = lax.broadcasted_iota(jnp.int32, (SLOTS, SLOTS), 0)
    slot = lax.broadcasted_iota(jnp.int32, (8, SLOTS), 1)
    list_ref[chunks:chunks + 8, :] = jnp.full((8, SLOTS), unused, jnp.int32)

    def compress(c, carry):
        at = position[pl.ds(c, 1), :]
        word = jnp.broadcast_to(packed[pl.ds(c, 1), :], (8, SLOTS))
        digits = (lax.shift_right_logical(word, shift) & 255).astype(jnp.float32).astype(jnp.bfloat16)
        chosen = jnp.where(place == at, 1.0, 0.0).astype(jnp.bfloat16)
        moved = lax.dot_general(digits, chosen, (((1,), (1,)), ((), ())), preferred_element_type=jnp.float32)
        whole = jnp.where(used, moved.astype(jnp.int32) << shift, 0)
        whole = jnp.sum(whole, axis=0, keepdims=True)
        total = jnp.max(jnp.broadcast_to(at, (8, SLOTS)), axis=1, keepdims=True) + 1
        list_ref[pl.ds(c, 1), :] = jnp.where(slot < total, jnp.broadcast_to(whole, (8, SLOTS)), unused)[0:1]
        return carry

    lax.fori_loop(0, chunks, compress, 0)

    def three(x):
        high = x.astype(jnp.bfloat16)
        left = x - high.astype(jnp.float32)
        middle = left.astype(jnp.bfloat16)
        return high, middle, (left - middle.astype(jnp.float32)).astype(jnp.bfloat16)

    def ones(shape, test):
        return jnp.where(
            test(lax.broadcasted_iota(jnp.int32, shape, 0), lax.broadcasted_iota(jnp.int32, shape, 1)), 1.0, 0.0
        ).astype(jnp.bfloat16)

    count = restrictions.shape[2]
    wide = ones((stalk, width), lambda p, q: p == q // channels)
    for j in range(stalk):
        total = jnp.zeros((count, width), jnp.float32)
        for part in three(restrictions[:, j, :]):
            total = total + lax.dot_general(part, wide, (((0,), (0,)), ((), ())), preferred_element_type=jnp.float32)
        for l in range(2):
            bank_ref[pl.ds(j // 8 * 16 + l * 8 + j % 8, count, stride=2 * stalk), :] = total[:, l * half:(l + 1) * half]

    tall = ones((width, channels), lambda p, q: (p & (channels - 1)) == q)
    broad = ones((channels, width), lambda p, q: p == (q & (channels - 1)))
    blocked = ones((width, width), lambda p, q: p // channels == q // channels)
    for k, part in enumerate(three(mixings[...])[:2]):
        part = jnp.dot(tall, part, preferred_element_type=jnp.float32).astype(jnp.bfloat16)
        spread_ref[k] = jnp.dot(part, broad, preferred_element_type=jnp.float32).astype(jnp.bfloat16) * blocked

    def widen(block, table, shard, k):
        def some(i, carry):
            at = pl.multiple_of(k * piece + i * 128, 128)
            rows_in = block[shard, pl.ds(at, 128), :].astype(jnp.float32)
            table[pl.ds(pl.multiple_of(shard * rows + at, 128), 128), :] = rows_in[:, 0:half]
            table[pl.ds(pl.multiple_of((reps + shard) * rows + at, 128), 128), :] = rows_in[:, half:width]
            return carry

        lax.fori_loop(0, piece // 128, some, 0)

    for k in every:
        to_mate_own[k].wait_recv()
        widen(own, near_table, rep, k)
        widen(own, near_table, mate, k)
    for k in every:
        to_pair_own[k].wait_recv()
        mate_pairs[k].start()
        if k in first:
            next_pairs[k].start()
        to_next_own[k].wait_recv()
        mate_lasts[k].start()
        if k in second:
            pair_lasts[k - PIECES // 2].start()
        widen(own, near_table, pair, k)
        widen(prev, far_table, pair, k)
        if k > 0:
            mate_pairs[k - 1].wait_recv()
            mate_lasts[k - 1].wait_recv()
            widen(own, near_table, far, k - 1)
            widen(prev, far_table, far, k - 1)
    for k in first:
        next_pairs[k].wait_recv()
        mate_rest[k].start()
        pair_lasts[k].wait_recv()
        mate_rest[k + PIECES // 2].start()
        if k == 0:
            mate_pairs[PIECES - 1].wait_recv()
            mate_lasts[PIECES - 1].wait_recv()
            widen(own, near_table, far, PIECES - 1)
            widen(prev, far_table, far, PIECES - 1)
        else:
            for j in (k - 1, k - 1 + PIECES // 2):
                mate_rest[j].wait_recv()
                widen(prev, far_table, mate, j)
        widen(prev, far_table, rep, k)
        widen(prev, far_table, rep, k + PIECES // 2)
    for j in (PIECES // 2 - 1, PIECES - 1):
        mate_rest[j].wait_recv()
        widen(prev, far_table, mate, j)
    for copy in index_copies:
        copy.wait_send()
    for family in (to_mate_own, to_pair_own, to_next_own, mate_pairs, mate_lasts, next_pairs, pair_lasts, mate_rest):
        for copy in family:
            copy.wait_send()


def exchange(dims, features, sources, targets, maps, counts, restriction, mixing):
    reps, blocks, rows, stalk, channels = dims
    width = stalk * channels
    chunks = reps * sources.size // SLOTS
    restriction = jnp.transpose(restriction, (1, 2, 0))
    operands = [pltpu.with_memory_space_constraint(x, pltpu.HBM) for x in (
        features, sources, targets, maps, counts, restriction, mixing)]
    vmem = pl.BlockSpec(memory_space=pltpu.VMEM)
    return pl.pallas_call(
        functools.partial(exchange_kernel, dims),
        out_shape=(
            pltpu.VMEM((reps, rows, width), features.dtype),
            pltpu.VMEM((reps, rows, width), features.dtype),
            pltpu.VMEM((2 * reps * rows, width // 2), jnp.float32),
            pltpu.VMEM((2 * reps * rows, width // 2), jnp.float32),
            pltpu.VMEM((chunks + 8, SLOTS), jnp.int32),
            pltpu.VMEM((chunks, 128), jnp.int32),
            pltpu.VMEM((2 * restriction.shape[2] * stalk, width // 2), jnp.float32),
            pltpu.VMEM((2, width, width), jnp.bfloat16),
        ),
        in_specs=[pl.BlockSpec(memory_space=pltpu.HBM)] * 7,
        out_specs=(vmem,) * 8,
        scratch_shapes=[
            pltpu.VMEM((reps, *sources.shape), jnp.int32),
            pltpu.VMEM((reps, *sources.shape), jnp.int32),
            pltpu.VMEM((reps, *sources.shape), jnp.int32),
            pltpu.VMEM((reps, *counts.shape), jnp.int32),
            pltpu.VMEM(restriction.shape, restriction.dtype),
            pltpu.VMEM(mixing.shape, mixing.dtype),
            pltpu.VMEM((chunks, SLOTS), jnp.int32),
            pltpu.VMEM((chunks, SLOTS), jnp.int32),
            pltpu.SemaphoreType.DMA((7,)),
            pltpu.SemaphoreType.DMA((4, 3)),
            pltpu.SemaphoreType.DMA((4, 3)),
            pltpu.SemaphoreType.DMA((8, PIECES)),
            pltpu.SemaphoreType.DMA((8, PIECES)),
        ],
        compiler_params=pltpu.CompilerParams(collective_id=0, has_side_effects=True, vmem_limit_bytes=8 << 20),
        name="exchange",
    )(*operands)


def column_sums(parts, sub):
    step = 1
    while len(parts) > 1:
        keep = (sub & step) == 0
        half = len(parts) // 2
        joined = []
        for a, b in zip(parts[:half], parts[half:]):
            joined.append(jnp.where(keep, a, b) + pltpu.roll(jnp.where(keep, b, a), step, 0))
        parts = joined
        step *= 2
    return parts[0]


def edge_kernel(dims, own_ref, near_table, far_table, list_ref, count_ref, bank_ref, spread_ref, out_ref,
                ring_even, ring_odd, starts, *rest):
    reps, rows, width, steps, chunks, slots = dims
    accs = rest
    half = width // 2
    rings = (ring_even, ring_odd)
    me = lax.axis_index("rep")
    def clear(i, _):
        at = pl.ds(pl.multiple_of(i * 128, 128), 128)
        for a in accs:
            a[at, :] = jnp.zeros((128, half), jnp.float32)
        return 0
    lax.fori_loop(0, accs[0].shape[0] // 128, clear, 0)
    sub = lax.broadcasted_iota(jnp.int32, (8, half), 0)
    diagonal = jnp.where(
        lax.broadcasted_iota(jnp.int32, (16, half), 1) // 16 == (lax.broadcasted_iota(jnp.int32, (16, half), 0) & 7), 1.0, 0.0
    ).astype(jnp.bfloat16)
    k_at = lax.broadcasted_iota(jnp.int32, (width, width), 0)
    n_at = lax.broadcasted_iota(jnp.int32, (width, width), 1)
    repeat = jnp.where((k_at % 16 == n_at % 16) & (k_at // half == n_at // half), 1.0, 0.0).astype(jnp.bfloat16)
    for turn in range(steps):
        table = (near_table, far_table)[turn]

        def plan(c, filled, turn=turn):
            at = c * steps + turn
            eights = (count_ref[at, 127] + 7) // 8

            def note(k, carry):
                starts[filled + k] = at * slots + 8 * k
                return carry

            lax.fori_loop(0, eights, note, 0)
            return filled + eights

        eights = lax.fori_loop(0, chunks // steps, plan, 0)
        for k in range(2 * EIGHTS):
            starts[eights + k] = chunks * slots
        groups = (eights + 2 * EIGHTS - 1) // (2 * EIGHTS)
        for k in range(2 * EIGHTS):
            starts[2 * EIGHTS * groups + k] = chunks * slots

        def words(g):
            found = []
            for k in range(EIGHTS):
                first = starts[g * EIGHTS + k]
                found += [list_ref[first + u] for u in range(8)]
            return found

        def load(now, sides, staged=None):
            for side in range(2):
                tiles = []
                for word in now[side * GROUP // 2:(side + 1) * GROUP // 2]:
                    src = word & 8191
                    both = jnp.concatenate(
                        [table[pl.ds(src, 8, stride=0), :], table[pl.ds(src + reps * rows, 8, stride=0), :]], axis=0)
                    tiles.append(both.astype(jnp.bfloat16) * diagonal)
                pairs = [jnp.concatenate(tiles[u:u + 2], axis=1) for u in range(0, GROUP // 2, 2)]
                pltpu.matmul_acc_lhs(sides[side], jnp.concatenate(pairs, axis=0), load_staged_rhs=staged)

        def add_up(now, popped, ring):
            for side in range(2):
                repeated = popped[side]
                for base in range(side * GROUP // 2, (side + 1) * GROUP // 2, 8):
                    lows, highs = [], []
                    for u in range(base, base + 8):
                        maps = bank_ref[pl.ds(pl.multiple_of((now[u] >> 8) & 2016, 32), 32), :]
                        row = u % (GROUP // 2) // 2 * 16
                        lane = u % 2 * half
                        top = repeated[row:row + 8, lane:lane + half]
                        low = repeated[row + 8:row + 16, lane:lane + half]
                        lows.append(maps[0:8] * top + maps[16:24] * low)
                        highs.append(maps[8:16] * top + maps[24:32] * low)
                    for k, parts in enumerate((lows, highs)):
                        message = column_sums([parts[i] for i in (0, 4, 2, 6, 1, 5, 3, 7)], sub)
                        ring[pl.ds(2 * base + k, 8, stride=2), :] = message.astype(jnp.bfloat16).astype(jnp.float32)
            for u in range(GROUP):
                acc = accs[u % ACCS]
                acc[pl.ds(lax.shift_right_logical(now[u], 19), 2), :] += ring[pl.ds(2 * u, 2), :]

        def run(*sides):
            even, odd = sides[:2], sides[2:]
            for side in range(2):
                pltpu.matmul_push_rhs(repeat, 0, side)
            load(words(0), even, 0)
            load(words(1), odd)

            def group(g, carry):
                for which, sides in enumerate((even, odd)):
                    popped = [pltpu.matmul_pop(side) for side in sides]
                    load(words(2 * g + which + 2), sides)
                    add_up(words(2 * g + which), popped, rings[which])
                return carry

            lax.fori_loop(0, groups, group, 0)
            for side in (*even, *odd):
                rings[0][0:8, :] = pltpu.matmul_pop(side)[0:8, 0:half]

        pl.run_scoped(run, *[pltpu.ACC(side)((4 * GROUP, width), jnp.float32) for side in (0, 1, 0, 1)])
    block = 128

    def finish(sides, i, carry):
        at = pl.ds(pl.multiple_of(i * block, block), block)
        halves = []
        for k in range(2):
            where = pl.ds(pl.multiple_of(i * 2 * block, 2 * block) + k, block, stride=2)
            side = accs[0][where, :]
            for a in accs[1:]:
                side = side + a[where, :]
            halves.append(side)
        total = jnp.concatenate(halves, axis=1)
        top = total.astype(jnp.bfloat16)
        low = (total - top.astype(jnp.float32)).astype(jnp.bfloat16)
        pltpu.matmul_acc_lhs(sides[0], top)
        pltpu.matmul_acc_lhs(sides[1], top)
        pltpu.matmul_acc_lhs(sides[0], low)
        mixed = pltpu.matmul_pop(sides[0]) + pltpu.matmul_pop(sides[1])
        own = own_ref[me, at, :].astype(jnp.float32)
        out_ref[at, :] = (own + mixed).astype(jnp.bfloat16)
        return carry

    def mix(*sides):
        blank = jnp.zeros((block, width), jnp.bfloat16)
        for side, weights in enumerate((spread_ref[0], spread_ref[1])):
            pltpu.matmul_push_rhs(weights, 0, side)
            pltpu.matmul_acc_lhs(sides[side], blank, load_staged_rhs=0)
        lax.fori_loop(0, rows // block, functools.partial(finish, sides), 0)

    pl.run_scoped(mix, *[pltpu.ACC(side)((block, width), jnp.float32) for side in range(2)])


def edges(own, near, far, lists, counts, bank, spread):
    reps, rows, width = own.shape
    chunks = counts.shape[0]
    dims = (reps, rows, width, 2, chunks, SLOTS)
    smem = pl.BlockSpec(memory_space=pltpu.SMEM)
    vmem = pl.BlockSpec(memory_space=pltpu.VMEM)
    return pl.pallas_call(
        functools.partial(edge_kernel, dims),
        out_shape=jax.ShapeDtypeStruct((rows, width), own.dtype),
        in_specs=[vmem, vmem, vmem, smem, smem, vmem, vmem],
        out_specs=vmem,
        scratch_shapes=[
            pltpu.VMEM((2 * GROUP, width // 2), jnp.float32),
            pltpu.VMEM((2 * GROUP, width // 2), jnp.float32),
            pltpu.SMEM((lists.shape[0] // 8 + 16,), jnp.int32),
            *[pltpu.VMEM((2 * rows + 128, width // 2), jnp.float32)] * ACCS,
        ],
        compiler_params=pltpu.CompilerParams(vmem_limit_bytes=16 << 20),
        name="edges",
    )(own, near, far, lists, counts, bank, spread)


def body(features, restriction, mixing, source_index, target_index, map_index, edge_counts):
    rows = features.shape[0]
    stalk = restriction.shape[1]
    channels = mixing.shape[0]
    dims = (lax.axis_size("rep"), lax.axis_size("blk"), rows, stalk, channels)
    own, _, near, far, lists, counts, bank, spread = exchange(
        dims, features, source_index, target_index, map_index, edge_counts, restriction, mixing)
    return edges(own, near, far, lists.reshape(-1), counts, bank, spread)


def solution(mesh):
    in_specs = (
        P(("blk", "rep"), None),
        P(),
        P(),
        P("blk", "rep", None, None),
        P("blk", "rep", None, None),
        P("blk", "rep", None, None),
        P("blk", "rep", None),
    )
    out_specs = P(("blk", "rep"), None)
    step = jax.shard_map(body, mesh=mesh, in_specs=in_specs, out_specs=out_specs, check_vma=False)

    def run(*args):
        with jax.sharding.use_abstract_mesh(mesh.abstract_mesh):
            return step(*args)

    return run
```

```python
import functools

import jax
import jax.numpy as jnp
from jax import lax
from jax.experimental import pallas as pl
from jax.experimental.pallas import tpu as pltpu
from jax.sharding import PartitionSpec as P

MESH = pl.DeviceIdType.MESH
PIECES = 4
SLOTS = 256
BLOCK = 8192
STARTS = 5
GROUP = 16
EIGHTS = GROUP // 8
ACCS = 4
FLIGHT = 4


def exchange_kernel(dims, features, source_ref, target_ref, map_ref, count_ref, restriction_ref, mixing_ref,
                    own, prev, near_table, far_table, list_ref, bank_ref, spread_ref,
                    sources, targets, maps, counts, restrictions, mixings, packed, position,
                    home_sem, index_send, index_recv, send, recv):
    reps, blocks, rows, stalk, channels = dims
    width = stalk * channels
    half = width // 2
    rep = lax.axis_index("rep")
    blk = lax.axis_index("blk")
    pair = lax.rem(rep + 2, 4)
    mate = rep + 1 - 2 * lax.rem(rep, 2)
    far = lax.rem(mate + 2, 4)
    after = lax.rem(blk + 1, blocks)
    before = lax.rem(blk + blocks - 1, blocks)
    to_mate = {"rep": mate, "blk": blk}
    to_pair = {"rep": pair, "blk": blk}
    to_next = {"rep": pair, "blk": after}
    from_last = {"rep": pair, "blk": before}

    home = [pltpu.make_async_copy(src, dst, home_sem.at[k]) for k, (src, dst) in enumerate((
        (source_ref, sources.at[rep]), (target_ref, targets.at[rep]), (map_ref, maps.at[rep]), (count_ref, counts.at[rep]),
        (features, own.at[rep]), (restriction_ref, restrictions), (mixing_ref, mixings)))]
    for copy in home:
        copy.start()

    barrier = pltpu.get_barrier_semaphore()
    for other in (to_mate, to_pair, to_next, from_last):
        pl.semaphore_signal(barrier, inc=1, device_id=other, device_id_type=MESH)
    pl.semaphore_wait(barrier, 4)

    index_copies = []
    for a, (src, dst) in enumerate(((source_ref, sources), (target_ref, targets), (map_ref, maps), (count_ref, counts))):
        for k, (part, place, other) in enumerate((
                (src, rep, to_mate), (src, rep, to_pair), (dst.at[pair], pair, to_mate))):
            index_copies.append(pltpu.make_async_remote_copy(
                src_ref=part, dst_ref=dst.at[place], send_sem=index_send.at[a, k], recv_sem=index_recv.at[a, k],
                device_id=other, device_id_type=MESH))
    for a in range(4):
        index_copies[3 * a + 1].start()
        index_copies[3 * a].start()

    piece = rows // PIECES

    def rows_of(k):
        return pl.ds(k * piece, piece)

    def remote(family, k, src, dst, other):
        return pltpu.make_async_remote_copy(
            src_ref=src, dst_ref=dst, send_sem=send.at[family, k], recv_sem=recv.at[family, k],
            device_id=other, device_id_type=MESH)

    every = range(PIECES)
    first, second = range(PIECES // 2), range(PIECES // 2, PIECES)
    to_mate_own = [remote(0, k, features.at[rows_of(k), :], own.at[rep, rows_of(k), :], to_mate) for k in every]
    to_pair_own = [remote(1, k, features.at[rows_of(k), :], own.at[rep, rows_of(k), :], to_pair) for k in every]
    to_next_own = [remote(2, k, features.at[rows_of(k), :], prev.at[rep, rows_of(k), :], to_next) for k in every]
    mate_pairs = [remote(3, k, own.at[pair, rows_of(k), :], own.at[pair, rows_of(k), :], to_mate) for k in every]
    mate_lasts = [remote(4, k, prev.at[pair, rows_of(k), :], prev.at[pair, rows_of(k), :], to_mate) for k in every]
    next_pairs = [remote(5, k, own.at[pair, rows_of(k), :], prev.at[pair, rows_of(k), :], to_next) for k in first]
    pair_lasts = [remote(6, k - PIECES // 2, prev.at[pair, rows_of(k), :], prev.at[pair, rows_of(k), :], to_pair) for k in second]
    mate_rest = [remote(7, k, prev.at[rep, rows_of(k), :], prev.at[rep, rows_of(k), :], to_mate) for k in every]

    for k in every:
        to_pair_own[k].start()
        to_next_own[k].start()
        to_mate_own[k].start()

    for copy in home:
        copy.wait()
    for a in range(4):
        index_copies[3 * a + 1].wait_recv()
        index_copies[3 * a + 2].start()
    for a in range(4):
        index_copies[3 * a].wait_recv()
        index_copies[3 * a + 2].wait_recv()
    steps, capacity = source_ref.shape[2:]
    runs = capacity // SLOTS
    chunks = reps * runs * steps
    spot = lax.broadcasted_iota(jnp.int32, (steps, SLOTS), 1)
    for r in range(reps):
        live = counts[r, 0]
        live = jnp.concatenate([jnp.broadcast_to(live[:, s:s + 1], (1, SLOTS)) for s in range(steps)], axis=0)
        for j in range(runs):
            part = pl.ds(j * SLOTS, SLOTS)
            to = sources.at[r, 0, 0, :, part][...]
            hit = targets.at[r, 0, 0, :, part][...]
            by = maps.at[r, 0, 0, :, part][...]
            here = (hit // rows == rep) & (spot + j * SLOTS < live)
            at = pl.ds((r * runs + j) * steps, steps)
            packed[at, :] = to + by * BLOCK + (hit & (rows - 1)) * (BLOCK * 128)
            position[at, :] = jnp.where(here, 1, 0)
    earlier = (lax.broadcasted_iota(jnp.int32, (SLOTS, SLOTS), 0) <= lax.broadcasted_iota(jnp.int32, (SLOTS, SLOTS), 1))
    here = position[...]
    running = jnp.dot(
        here.astype(jnp.float32).astype(jnp.bfloat16), earlier.astype(jnp.float32).astype(jnp.bfloat16),
        preferred_element_type=jnp.float32).astype(jnp.int32)
    eights = (running[:, SLOTS - 1:SLOTS] + 7) // 8
    chunk_of = lax.broadcasted_iota(jnp.int32, (chunks, 1), 0)
    ahead = jnp.where(
        lax.broadcasted_iota(jnp.int32, (chunks, chunks), 1) < lax.broadcasted_iota(jnp.int32, (chunks, chunks), 0), 1.0, 0.0)
    run = lax.broadcasted_iota(jnp.int32, (chunks, STARTS * SLOTS), 1)
    for t in range(steps):
        mine = jnp.where(chunk_of % steps == t, eights, 0)
        mine_wide = jnp.broadcast_to(mine, (chunks, SLOTS))
        begun = jnp.dot(
            ahead.astype(jnp.bfloat16), mine_wide.astype(jnp.float32).astype(jnp.bfloat16),
            preferred_element_type=jnp.float32).astype(jnp.int32)[:, 0:1]
        inside = (run >= begun) & (run < begun + mine)
        table_row = jnp.sum(
            jnp.where(inside, (chunk_of - chunks) * SLOTS + 8 * (run - begun), 0), axis=0, keepdims=True) + chunks * SLOTS
        to = chunks + 8 + 8 * t
        for k in range(STARTS):
            list_ref[to + k:to + k + 1, :] = table_row[:, k * SLOTS:(k + 1) * SLOTS]
        list_ref[to + STARTS:to + STARTS + 1, :] = jnp.sum(mine_wide, axis=0, keepdims=True)
    position[...] = jnp.where(here > 0, running - 1, -1)
    unused = rows * (BLOCK * 128) - 2**32
    shift = 8 * jnp.minimum(lax.broadcasted_iota(jnp.int32, (8, SLOTS), 0), 3)
    used = lax.broadcasted_iota(jnp.int32, (8, SLOTS), 0) < 4
    place = lax.broadcasted_iota(jnp.int32, (SLOTS, SLOTS), 0)
    slot = lax.broadcasted_iota(jnp.int32, (8, SLOTS), 1)
    list_ref[chunks:chunks + 8, :] = jnp.full((8, SLOTS), unused, jnp.int32)

    def compress(c, carry):
        at = position[pl.ds(c, 1), :]
        word = jnp.broadcast_to(packed[pl.ds(c, 1), :], (8, SLOTS))
        digits = (lax.shift_right_logical(word, shift) & 255).astype(jnp.float32).astype(jnp.bfloat16)
        chosen = jnp.where(place == at, 1.0, 0.0).astype(jnp.bfloat16)
        moved = lax.dot_general(digits, chosen, (((1,), (1,)), ((), ())), preferred_element_type=jnp.float32)
        whole = jnp.where(used, moved.astype(jnp.int32) << shift, 0)
        whole = jnp.sum(whole, axis=0, keepdims=True)
        total = jnp.max(jnp.broadcast_to(at, (8, SLOTS)), axis=1, keepdims=True) + 1
        list_ref[pl.ds(c, 1), :] = jnp.where(slot < total, jnp.broadcast_to(whole, (8, SLOTS)), unused)[0:1]
        return carry

    lax.fori_loop(0, chunks, compress, 0)

    def three(x):
        high = x.astype(jnp.bfloat16)
        left = x - high.astype(jnp.float32)
        middle = left.astype(jnp.bfloat16)
        return high, middle, (left - middle.astype(jnp.float32)).astype(jnp.bfloat16)

    def ones(shape, test):
        return jnp.where(
            test(lax.broadcasted_iota(jnp.int32, shape, 0), lax.broadcasted_iota(jnp.int32, shape, 1)), 1.0, 0.0
        ).astype(jnp.bfloat16)

    count = restrictions.shape[2]
    wide = ones((stalk, width), lambda p, q: p == q // channels)
    for j in range(stalk):
        total = jnp.zeros((count, width), jnp.float32)
        for part in three(restrictions[:, j, :]):
            total = total + lax.dot_general(part, wide, (((0,), (0,)), ((), ())), preferred_element_type=jnp.float32)
        for l in range(2):
            bank_ref[pl.ds(j // 8 * 16 + l * 8 + j % 8, count, stride=2 * stalk), :] = total[:, l * half:(l + 1) * half]

    tall = ones((width, channels), lambda p, q: (p & (channels - 1)) == q)
    broad = ones((channels, width), lambda p, q: p == (q & (channels - 1)))
    blocked = ones((width, width), lambda p, q: p // channels == q // channels)
    for k, part in enumerate(three(mixings[...])[:2]):
        part = jnp.dot(tall, part, preferred_element_type=jnp.float32).astype(jnp.bfloat16)
        spread_ref[k] = jnp.dot(part, broad, preferred_element_type=jnp.float32).astype(jnp.bfloat16) * blocked

    def widen(block, table, shard, k):
        def some(i, carry):
            at = pl.multiple_of(k * piece + i * 128, 128)
            rows_in = block[shard, pl.ds(at, 128), :].astype(jnp.float32)
            table[pl.ds(pl.multiple_of(shard * rows + at, 128), 128), :] = rows_in[:, 0:half]
            table[pl.ds(pl.multiple_of((reps + shard) * rows + at, 128), 128), :] = rows_in[:, half:width]
            return carry

        lax.fori_loop(0, piece // 128, some, 0)

    for k in every:
        to_mate_own[k].wait_recv()
        widen(own, near_table, rep, k)
        widen(own, near_table, mate, k)
    for k in every:
        to_pair_own[k].wait_recv()
        mate_pairs[k].start()
        if k in first:
            next_pairs[k].start()
        to_next_own[k].wait_recv()
        mate_lasts[k].start()
        if k in second:
            pair_lasts[k - PIECES // 2].start()
        widen(own, near_table, pair, k)
        widen(prev, far_table, pair, k)
        if k > 0:
            mate_pairs[k - 1].wait_recv()
            mate_lasts[k - 1].wait_recv()
            widen(own, near_table, far, k - 1)
            widen(prev, far_table, far, k - 1)
    for k in first:
        next_pairs[k].wait_recv()
        mate_rest[k].start()
        pair_lasts[k].wait_recv()
        mate_rest[k + PIECES // 2].start()
        if k == 0:
            mate_pairs[PIECES - 1].wait_recv()
            mate_lasts[PIECES - 1].wait_recv()
            widen(own, near_table, far, PIECES - 1)
            widen(prev, far_table, far, PIECES - 1)
        else:
            for j in (k - 1, k - 1 + PIECES // 2):
                mate_rest[j].wait_recv()
                widen(prev, far_table, mate, j)
        widen(prev, far_table, rep, k)
        widen(prev, far_table, rep, k + PIECES // 2)
    for j in (PIECES // 2 - 1, PIECES - 1):
        mate_rest[j].wait_recv()
        widen(prev, far_table, mate, j)
    for copy in index_copies:
        copy.wait_send()
    for family in (to_mate_own, to_pair_own, to_next_own, mate_pairs, mate_lasts, next_pairs, pair_lasts, mate_rest):
        for copy in family:
            copy.wait_send()


def exchange(dims, features, sources, targets, maps, counts, restriction, mixing):
    reps, blocks, rows, stalk, channels = dims
    width = stalk * channels
    chunks = reps * sources.size // SLOTS
    restriction = jnp.transpose(restriction, (1, 2, 0))
    operands = [pltpu.with_memory_space_constraint(x, pltpu.HBM) for x in (
        features, sources, targets, maps, counts, restriction, mixing)]
    vmem = pl.BlockSpec(memory_space=pltpu.VMEM)
    return pl.pallas_call(
        functools.partial(exchange_kernel, dims),
        out_shape=(
            pltpu.VMEM((reps, rows, width), features.dtype),
            pltpu.VMEM((reps, rows, width), features.dtype),
            pltpu.VMEM((2 * reps * rows, width // 2), jnp.float32),
            pltpu.VMEM((2 * reps * rows, width // 2), jnp.float32),
            pltpu.VMEM((chunks + 24, SLOTS), jnp.int32),
            pltpu.VMEM((2 * restriction.shape[2] * stalk, width // 2), jnp.float32),
            pltpu.VMEM((2, width, width), jnp.bfloat16),
        ),
        in_specs=[pl.BlockSpec(memory_space=pltpu.HBM)] * 7,
        out_specs=(vmem,) * 7,
        scratch_shapes=[
            pltpu.VMEM((reps, *sources.shape), jnp.int32),
            pltpu.VMEM((reps, *sources.shape), jnp.int32),
            pltpu.VMEM((reps, *sources.shape), jnp.int32),
            pltpu.VMEM((reps, *counts.shape), jnp.int32),
            pltpu.VMEM(restriction.shape, restriction.dtype),
            pltpu.VMEM(mixing.shape, mixing.dtype),
            pltpu.VMEM((chunks, SLOTS), jnp.int32),
            pltpu.VMEM((chunks, SLOTS), jnp.int32),
            pltpu.SemaphoreType.DMA((7,)),
            pltpu.SemaphoreType.DMA((4, 3)),
            pltpu.SemaphoreType.DMA((4, 3)),
            pltpu.SemaphoreType.DMA((8, PIECES)),
            pltpu.SemaphoreType.DMA((8, PIECES)),
        ],
        compiler_params=pltpu.CompilerParams(collective_id=0, has_side_effects=True, vmem_limit_bytes=8 << 20),
        name="exchange",
    )(*operands)


def column_sums(parts, sub):
    step = 1
    while len(parts) > 1:
        keep = (sub & step) == 0
        half = len(parts) // 2
        joined = []
        for a, b in zip(parts[:half], parts[half:]):
            joined.append(jnp.where(keep, a, b) + pltpu.roll(jnp.where(keep, b, a), step, 0))
        parts = joined
        step *= 2
    return parts[0]


def edge_kernel(dims, own_ref, near_table, far_table, list_ref, bank_ref, spread_ref, out_ref,
                ring_even, ring_odd, *rest):
    reps, rows, width, steps, chunks, slots = dims
    accs = rest
    half = width // 2
    rings = (ring_even, ring_odd)
    me = lax.axis_index("rep")
    def clear(i, _):
        at = pl.ds(pl.multiple_of(i * 128, 128), 128)
        for a in accs:
            a[at, :] = jnp.zeros((128, half), jnp.float32)
        return 0
    lax.fori_loop(0, accs[0].shape[0] // 128, clear, 0)
    sub = lax.broadcasted_iota(jnp.int32, (8, half), 0)
    diagonal = jnp.where(
        lax.broadcasted_iota(jnp.int32, (16, half), 1) // 16 == (lax.broadcasted_iota(jnp.int32, (16, half), 0) & 7), 1.0, 0.0
    ).astype(jnp.bfloat16)
    k_at = lax.broadcasted_iota(jnp.int32, (width, width), 0)
    n_at = lax.broadcasted_iota(jnp.int32, (width, width), 1)
    repeat = jnp.where((k_at % 16 == n_at % 16) & (k_at // half == n_at // half), 1.0, 0.0).astype(jnp.bfloat16)
    for turn in range(steps):
        table = (near_table, far_table)[turn]

        starts = (chunks + 8 + 8 * turn) * slots
        groups = (list_ref[starts + STARTS * slots] + 2 * EIGHTS - 1) // (2 * EIGHTS)

        def words(g):
            found = []
            for k in range(EIGHTS):
                eight = list_ref.at[pl.ds(list_ref[starts + g * EIGHTS + k], 8)]
                found += [eight[u] for u in range(8)]
            return found

        def load(now, sides, staged=None):
            for side in range(2):
                tiles = []
                for word in now[side * GROUP // 2:(side + 1) * GROUP // 2]:
                    src = word & 8191
                    both = jnp.concatenate(
                        [table[pl.ds(src, 8, stride=0), :], table[pl.ds(src + reps * rows, 8, stride=0), :]], axis=0)
                    tiles.append(both.astype(jnp.bfloat16) * diagonal)
                pairs = [jnp.concatenate(tiles[u:u + 2], axis=1) for u in range(0, GROUP // 2, 2)]
                pltpu.matmul_acc_lhs(sides[side], jnp.concatenate(pairs, axis=0), load_staged_rhs=staged)

        def add_up(now, popped, ring):
            for side in range(2):
                repeated = popped[side]
                for base in range(side * GROUP // 2, (side + 1) * GROUP // 2, 8):
                    lows, highs = [], []
                    for u in range(base, base + 8):
                        maps = bank_ref[pl.ds(pl.multiple_of((now[u] >> 8) & 2016, 32), 32), :]
                        row = u % (GROUP // 2) // 2 * 16
                        lane = u % 2 * half
                        top = repeated[row:row + 8, lane:lane + half]
                        low = repeated[row + 8:row + 16, lane:lane + half]
                        lows.append(maps[0:8] * top + maps[16:24] * low)
                        highs.append(maps[8:16] * top + maps[24:32] * low)
                    for k, parts in enumerate((lows, highs)):
                        message = column_sums([parts[i] for i in (0, 4, 2, 6, 1, 5, 3, 7)], sub)
                        ring[pl.ds(2 * base + k, 8, stride=2), :] = message.astype(jnp.bfloat16).astype(jnp.float32)
            for u in range(GROUP):
                acc = accs[u % ACCS]
                acc[pl.ds(lax.shift_right_logical(now[u], 19), 2), :] += ring[pl.ds(2 * u, 2), :]

        def run(*sides):
            even, odd = sides[:2], sides[2:]
            for side in range(2):
                pltpu.matmul_push_rhs(repeat, 0, side)
            load(words(0), even, 0)
            load(words(1), odd)

            def group(g, carry):
                for which, sides in enumerate((even, odd)):
                    popped = [pltpu.matmul_pop(side) for side in sides]
                    load(words(2 * g + which + 2), sides)
                    add_up(words(2 * g + which), popped, rings[which])
                return carry

            lax.fori_loop(0, groups, group, 0)
            for side in (*even, *odd):
                rings[0][0:8, :] = pltpu.matmul_pop(side)[0:8, 0:half]

        pl.run_scoped(run, *[pltpu.ACC(side)((4 * GROUP, width), jnp.float32) for side in (0, 1, 0, 1)])
    block = 64

    def begin(i, sides):
        halves = []
        for k in range(2):
            where = pl.ds(pl.multiple_of(i * 2 * block, 2 * block) + k, block, stride=2)
            side = accs[0][where, :]
            for a in accs[1:]:
                side = side + a[where, :]
            halves.append(side)
        total = jnp.concatenate(halves, axis=1)
        top = total.astype(jnp.bfloat16)
        low = (total - top.astype(jnp.float32)).astype(jnp.bfloat16)
        pltpu.matmul_acc_lhs(sides[0], top)
        pltpu.matmul_acc_lhs(sides[1], top)
        pltpu.matmul_acc_lhs(sides[0], low)

    def end(i, sides):
        at = pl.ds(pl.multiple_of(i * block, block), block)
        mixed = pltpu.matmul_pop(sides[0]) + pltpu.matmul_pop(sides[1])
        out_ref[at, :] = (own_ref[me, at, :].astype(jnp.float32) + mixed).astype(jnp.bfloat16)

    def mix(*sides):
        lanes = [sides[2 * k:2 * k + 2] for k in range(FLIGHT)]
        blank = jnp.zeros((block, width), jnp.bfloat16)
        for side in range(2):
            pltpu.matmul_push_rhs(spread_ref[side], 0, side)
            pltpu.matmul_acc_lhs(sides[side], blank, load_staged_rhs=0)
        blocks = rows // block
        for k in range(FLIGHT):
            begin(k, lanes[k])

        def some(i, carry):
            for k in range(FLIGHT):
                end(i * FLIGHT + k, lanes[k])
                begin((i + 1) * FLIGHT + k, lanes[k])
            return carry

        lax.fori_loop(0, blocks // FLIGHT - 1, some, 0)
        for k in range(FLIGHT):
            end(blocks - FLIGHT + k, lanes[k])

    pl.run_scoped(mix, *[pltpu.ACC(side)((block, width), jnp.float32) for side in (0, 1) * FLIGHT])


def edges(own, near, far, lists, bank, spread):
    reps, rows, width = own.shape
    chunks = lists.shape[0] // SLOTS - 24
    dims = (reps, rows, width, 2, chunks, SLOTS)
    smem = pl.BlockSpec(memory_space=pltpu.SMEM)
    vmem = pl.BlockSpec(memory_space=pltpu.VMEM)
    return pl.pallas_call(
        functools.partial(edge_kernel, dims),
        out_shape=jax.ShapeDtypeStruct((rows, width), own.dtype),
        in_specs=[vmem, vmem, vmem, smem, vmem, vmem],
        out_specs=vmem,
        scratch_shapes=[
            pltpu.VMEM((2 * GROUP, width // 2), jnp.float32),
            pltpu.VMEM((2 * GROUP, width // 2), jnp.float32),
            *[pltpu.VMEM((2 * rows + 128, width // 2), jnp.float32)] * ACCS,
        ],
        compiler_params=pltpu.CompilerParams(vmem_limit_bytes=16 << 20),
        name="edges",
    )(own, near, far, lists, bank, spread)


def body(features, restriction, mixing, source_index, target_index, map_index, edge_counts):
    rows = features.shape[0]
    stalk = restriction.shape[1]
    channels = mixing.shape[0]
    dims = (lax.axis_size("rep"), lax.axis_size("blk"), rows, stalk, channels)
    own, _, near, far, lists, bank, spread = exchange(
        dims, features, source_index, target_index, map_index, edge_counts, restriction, mixing)
    return edges(own, near, far, lists.reshape(-1), bank, spread)


def solution(mesh):
    in_specs = (
        P(("blk", "rep"), None),
        P(),
        P(),
        P("blk", "rep", None, None),
        P("blk", "rep", None, None),
        P("blk", "rep", None, None),
        P("blk", "rep", None),
    )
    out_specs = P(("blk", "rep"), None)
    step = jax.shard_map(body, mesh=mesh, in_specs=in_specs, out_specs=out_specs, check_vma=False)

    def run(*args):
        with jax.sharding.use_abstract_mesh(mesh.abstract_mesh):
            return step(*args)

    return run
```

```python
import functools

import jax
import jax.numpy as jnp
from jax import lax
from jax.experimental import pallas as pl
from jax.experimental.pallas import tpu as pltpu
from jax.sharding import PartitionSpec as P

MESH = pl.DeviceIdType.MESH
PIECES = 4
SLOTS = 256
BLOCK = 8192
STARTS = 5
GROUP = 48
EIGHTS = GROUP // 8
ACCS = 4
FLIGHT = 4


def exchange_kernel(dims, features, source_ref, target_ref, map_ref, count_ref, restriction_ref, mixing_ref,
                    own, prev, near_table, far_table, list_ref, bank_ref, spread_ref,
                    sources, targets, maps, counts, restrictions, mixings, packed, position,
                    home_sem, index_send, index_recv, send, recv):
    reps, blocks, rows, stalk, channels = dims
    width = stalk * channels
    half = width // 2
    rep = lax.axis_index("rep")
    blk = lax.axis_index("blk")
    pair = lax.rem(rep + 2, 4)
    mate = rep + 1 - 2 * lax.rem(rep, 2)
    far = lax.rem(mate + 2, 4)
    after = lax.rem(blk + 1, blocks)
    before = lax.rem(blk + blocks - 1, blocks)
    to_mate = {"rep": mate, "blk": blk}
    to_pair = {"rep": pair, "blk": blk}
    to_next = {"rep": pair, "blk": after}
    from_last = {"rep": pair, "blk": before}

    home = [pltpu.make_async_copy(src, dst, home_sem.at[k]) for k, (src, dst) in enumerate((
        (source_ref, sources.at[rep]), (target_ref, targets.at[rep]), (map_ref, maps.at[rep]), (count_ref, counts.at[rep]),
        (features, own.at[rep]), (restriction_ref, restrictions), (mixing_ref, mixings)))]
    for copy in home:
        copy.start()

    barrier = pltpu.get_barrier_semaphore()
    for other in (to_mate, to_pair, to_next, from_last):
        pl.semaphore_signal(barrier, inc=1, device_id=other, device_id_type=MESH)
    pl.semaphore_wait(barrier, 4)

    index_copies = []
    for a, (src, dst) in enumerate(((source_ref, sources), (target_ref, targets), (map_ref, maps), (count_ref, counts))):
        for k, (part, place, other) in enumerate((
                (src, rep, to_mate), (src, rep, to_pair), (dst.at[pair], pair, to_mate))):
            index_copies.append(pltpu.make_async_remote_copy(
                src_ref=part, dst_ref=dst.at[place], send_sem=index_send.at[a, k], recv_sem=index_recv.at[a, k],
                device_id=other, device_id_type=MESH))
    for a in range(4):
        index_copies[3 * a + 1].start()
        index_copies[3 * a].start()

    piece = rows // PIECES

    def rows_of(k):
        return pl.ds(k * piece, piece)

    def remote(family, k, src, dst, other):
        return pltpu.make_async_remote_copy(
            src_ref=src, dst_ref=dst, send_sem=send.at[family, k], recv_sem=recv.at[family, k],
            device_id=other, device_id_type=MESH)

    every = range(PIECES)
    first, second = range(PIECES // 2), range(PIECES // 2, PIECES)
    to_mate_own = [remote(0, k, features.at[rows_of(k), :], own.at[rep, rows_of(k), :], to_mate) for k in every]
    to_pair_own = [remote(1, k, features.at[rows_of(k), :], own.at[rep, rows_of(k), :], to_pair) for k in every]
    to_next_own = [remote(2, k, features.at[rows_of(k), :], prev.at[rep, rows_of(k), :], to_next) for k in every]
    mate_pairs = [remote(3, k, own.at[pair, rows_of(k), :], own.at[pair, rows_of(k), :], to_mate) for k in every]
    mate_lasts = [remote(4, k, prev.at[pair, rows_of(k), :], prev.at[pair, rows_of(k), :], to_mate) for k in every]
    next_pairs = [remote(5, k, own.at[pair, rows_of(k), :], prev.at[pair, rows_of(k), :], to_next) for k in first]
    pair_lasts = [remote(6, k - PIECES // 2, prev.at[pair, rows_of(k), :], prev.at[pair, rows_of(k), :], to_pair) for k in second]
    mate_rest = [remote(7, k, prev.at[rep, rows_of(k), :], prev.at[rep, rows_of(k), :], to_mate) for k in every]

    for k in every:
        to_pair_own[k].start()
        to_next_own[k].start()
        to_mate_own[k].start()

    for copy in home:
        copy.wait()
    for a in range(4):
        index_copies[3 * a + 1].wait_recv()
        index_copies[3 * a + 2].start()
    for a in range(4):
        index_copies[3 * a].wait_recv()
        index_copies[3 * a + 2].wait_recv()
    steps, capacity = source_ref.shape[2:]
    runs = capacity // SLOTS
    chunks = reps * runs * steps
    spot = lax.broadcasted_iota(jnp.int32, (steps, SLOTS), 1)
    for r in range(reps):
        live = counts[r, 0]
        live = jnp.concatenate([jnp.broadcast_to(live[:, s:s + 1], (1, SLOTS)) for s in range(steps)], axis=0)
        for j in range(runs):
            part = pl.ds(j * SLOTS, SLOTS)
            to = sources.at[r, 0, 0, :, part][...]
            hit = targets.at[r, 0, 0, :, part][...]
            by = maps.at[r, 0, 0, :, part][...]
            here = (hit // rows == rep) & (spot + j * SLOTS < live)
            at = pl.ds((r * runs + j) * steps, steps)
            packed[at, :] = to + by * BLOCK + (hit & (rows - 1)) * (BLOCK * 128)
            position[at, :] = jnp.where(here, 1, 0)
    earlier = (lax.broadcasted_iota(jnp.int32, (SLOTS, SLOTS), 0) <= lax.broadcasted_iota(jnp.int32, (SLOTS, SLOTS), 1))
    here = position[...]
    running = jnp.dot(
        here.astype(jnp.float32).astype(jnp.bfloat16), earlier.astype(jnp.float32).astype(jnp.bfloat16),
        preferred_element_type=jnp.float32).astype(jnp.int32)
    eights = (running[:, SLOTS - 1:SLOTS] + 7) // 8
    chunk_of = lax.broadcasted_iota(jnp.int32, (chunks, 1), 0)
    ahead = jnp.where(
        lax.broadcasted_iota(jnp.int32, (chunks, chunks), 1) < lax.broadcasted_iota(jnp.int32, (chunks, chunks), 0), 1.0, 0.0)
    run = lax.broadcasted_iota(jnp.int32, (chunks, STARTS * SLOTS), 1)
    for t in range(steps):
        mine = jnp.where(chunk_of % steps == t, eights, 0)
        mine_wide = jnp.broadcast_to(mine, (chunks, SLOTS))
        begun = jnp.dot(
            ahead.astype(jnp.bfloat16), mine_wide.astype(jnp.float32).astype(jnp.bfloat16),
            preferred_element_type=jnp.float32).astype(jnp.int32)[:, 0:1]
        inside = (run >= begun) & (run < begun + mine)
        table_row = jnp.sum(
            jnp.where(inside, (chunk_of - chunks) * SLOTS + 8 * (run - begun), 0), axis=0, keepdims=True) + chunks * SLOTS
        to = chunks + 8 + 8 * t
        for k in range(STARTS):
            list_ref[to + k:to + k + 1, :] = table_row[:, k * SLOTS:(k + 1) * SLOTS]
        list_ref[to + STARTS:to + STARTS + 1, :] = jnp.sum(mine_wide, axis=0, keepdims=True)
    position[...] = jnp.where(here > 0, running - 1, -1)
    unused = rows * (BLOCK * 128) - 2**32
    shift = 8 * jnp.minimum(lax.broadcasted_iota(jnp.int32, (8, SLOTS), 0), 3)
    used = lax.broadcasted_iota(jnp.int32, (8, SLOTS), 0) < 4
    place = lax.broadcasted_iota(jnp.int32, (SLOTS, SLOTS), 0)
    slot = lax.broadcasted_iota(jnp.int32, (8, SLOTS), 1)
    list_ref[chunks:chunks + 8, :] = jnp.full((8, SLOTS), unused, jnp.int32)

    def compress(c, carry):
        at = position[pl.ds(c, 1), :]
        word = jnp.broadcast_to(packed[pl.ds(c, 1), :], (8, SLOTS))
        digits = (lax.shift_right_logical(word, shift) & 255).astype(jnp.float32).astype(jnp.bfloat16)
        chosen = jnp.where(place == at, 1.0, 0.0).astype(jnp.bfloat16)
        moved = lax.dot_general(digits, chosen, (((1,), (1,)), ((), ())), preferred_element_type=jnp.float32)
        whole = jnp.where(used, moved.astype(jnp.int32) << shift, 0)
        whole = jnp.sum(whole, axis=0, keepdims=True)
        total = jnp.max(jnp.broadcast_to(at, (8, SLOTS)), axis=1, keepdims=True) + 1
        list_ref[pl.ds(c, 1), :] = jnp.where(slot < total, jnp.broadcast_to(whole, (8, SLOTS)), unused)[0:1]
        return carry

    lax.fori_loop(0, chunks, compress, 0)

    def three(x):
        high = x.astype(jnp.bfloat16)
        left = x - high.astype(jnp.float32)
        middle = left.astype(jnp.bfloat16)
        return high, middle, (left - middle.astype(jnp.float32)).astype(jnp.bfloat16)

    def ones(shape, test):
        return jnp.where(
            test(lax.broadcasted_iota(jnp.int32, shape, 0), lax.broadcasted_iota(jnp.int32, shape, 1)), 1.0, 0.0
        ).astype(jnp.bfloat16)

    count = restrictions.shape[2]
    wide = ones((stalk, width), lambda p, q: p == q // channels)
    for j in range(stalk):
        total = jnp.zeros((count, width), jnp.float32)
        for part in three(restrictions[:, j, :]):
            total = total + lax.dot_general(part, wide, (((0,), (0,)), ((), ())), preferred_element_type=jnp.float32)
        for l in range(2):
            bank_ref[pl.ds(j // 8 * 16 + l * 8 + j % 8, count, stride=2 * stalk), :] = total[:, l * half:(l + 1) * half]

    tall = ones((width, channels), lambda p, q: (p & (channels - 1)) == q)
    broad = ones((channels, width), lambda p, q: p == (q & (channels - 1)))
    blocked = ones((width, width), lambda p, q: p // channels == q // channels)
    for k, part in enumerate(three(mixings[...])[:2]):
        part = jnp.dot(tall, part, preferred_element_type=jnp.float32).astype(jnp.bfloat16)
        spread_ref[k] = jnp.dot(part, broad, preferred_element_type=jnp.float32).astype(jnp.bfloat16) * blocked

    def widen(block, table, shard, k):
        def some(i, carry):
            at = pl.multiple_of(k * piece + i * 128, 128)
            rows_in = block[shard, pl.ds(at, 128), :].astype(jnp.float32)
            table[pl.ds(pl.multiple_of(shard * rows + at, 128), 128), :] = rows_in[:, 0:half]
            table[pl.ds(pl.multiple_of((reps + shard) * rows + at, 128), 128), :] = rows_in[:, half:width]
            return carry

        lax.fori_loop(0, piece // 128, some, 0)

    for k in every:
        to_mate_own[k].wait_recv()
        widen(own, near_table, rep, k)
        widen(own, near_table, mate, k)
    for k in every:
        to_pair_own[k].wait_recv()
        mate_pairs[k].start()
        if k in first:
            next_pairs[k].start()
        to_next_own[k].wait_recv()
        mate_lasts[k].start()
        if k in second:
            pair_lasts[k - PIECES // 2].start()
        widen(own, near_table, pair, k)
        widen(prev, far_table, pair, k)
        if k > 0:
            mate_pairs[k - 1].wait_recv()
            mate_lasts[k - 1].wait_recv()
            widen(own, near_table, far, k - 1)
            widen(prev, far_table, far, k - 1)
    for k in first:
        next_pairs[k].wait_recv()
        mate_rest[k].start()
        pair_lasts[k].wait_recv()
        mate_rest[k + PIECES // 2].start()
        if k == 0:
            mate_pairs[PIECES - 1].wait_recv()
            mate_lasts[PIECES - 1].wait_recv()
            widen(own, near_table, far, PIECES - 1)
            widen(prev, far_table, far, PIECES - 1)
        else:
            for j in (k - 1, k - 1 + PIECES // 2):
                mate_rest[j].wait_recv()
                widen(prev, far_table, mate, j)
        widen(prev, far_table, rep, k)
        widen(prev, far_table, rep, k + PIECES // 2)
    for j in (PIECES // 2 - 1, PIECES - 1):
        mate_rest[j].wait_recv()
        widen(prev, far_table, mate, j)
    for copy in index_copies:
        copy.wait_send()
    for family in (to_mate_own, to_pair_own, to_next_own, mate_pairs, mate_lasts, next_pairs, pair_lasts, mate_rest):
        for copy in family:
            copy.wait_send()


def exchange(dims, features, sources, targets, maps, counts, restriction, mixing):
    reps, blocks, rows, stalk, channels = dims
    width = stalk * channels
    chunks = reps * sources.size // SLOTS
    restriction = jnp.transpose(restriction, (1, 2, 0))
    operands = [pltpu.with_memory_space_constraint(x, pltpu.HBM) for x in (
        features, sources, targets, maps, counts, restriction, mixing)]
    vmem = pl.BlockSpec(memory_space=pltpu.VMEM)
    return pl.pallas_call(
        functools.partial(exchange_kernel, dims),
        out_shape=(
            pltpu.VMEM((reps, rows, width), features.dtype),
            pltpu.VMEM((reps, rows, width), features.dtype),
            pltpu.VMEM((2 * reps * rows, width // 2), jnp.float32),
            pltpu.VMEM((2 * reps * rows, width // 2), jnp.float32),
            pltpu.VMEM((chunks + 24, SLOTS), jnp.int32),
            pltpu.VMEM((2 * restriction.shape[2] * stalk, width // 2), jnp.float32),
            pltpu.VMEM((2, width, width), jnp.bfloat16),
        ),
        in_specs=[pl.BlockSpec(memory_space=pltpu.HBM)] * 7,
        out_specs=(vmem,) * 7,
        scratch_shapes=[
            pltpu.VMEM((reps, *sources.shape), jnp.int32),
            pltpu.VMEM((reps, *sources.shape), jnp.int32),
            pltpu.VMEM((reps, *sources.shape), jnp.int32),
            pltpu.VMEM((reps, *counts.shape), jnp.int32),
            pltpu.VMEM(restriction.shape, restriction.dtype),
            pltpu.VMEM(mixing.shape, mixing.dtype),
            pltpu.VMEM((chunks, SLOTS), jnp.int32),
            pltpu.VMEM((chunks, SLOTS), jnp.int32),
            pltpu.SemaphoreType.DMA((7,)),
            pltpu.SemaphoreType.DMA((4, 3)),
            pltpu.SemaphoreType.DMA((4, 3)),
            pltpu.SemaphoreType.DMA((8, PIECES)),
            pltpu.SemaphoreType.DMA((8, PIECES)),
        ],
        compiler_params=pltpu.CompilerParams(collective_id=0, has_side_effects=True, vmem_limit_bytes=8 << 20),
        name="exchange",
    )(*operands)


def column_sums(parts, sub):
    step = 1
    while len(parts) > 1:
        keep = (sub & step) == 0
        half = len(parts) // 2
        joined = []
        for a, b in zip(parts[:half], parts[half:]):
            joined.append(jnp.where(keep, a, b) + pltpu.roll(jnp.where(keep, b, a), step, 0))
        parts = joined
        step *= 2
    return parts[0]


def edge_kernel(dims, own_ref, near_table, far_table, list_ref, bank_ref, spread_ref, out_ref,
                ring_even, ring_odd, *rest):
    reps, rows, width, steps, chunks, slots = dims
    accs = rest
    half = width // 2
    rings = (ring_even, ring_odd)
    me = lax.axis_index("rep")
    def clear(i, _):
        at = pl.ds(pl.multiple_of(i * 128, 128), 128)
        for a in accs:
            a[at, :] = jnp.zeros((128, half), jnp.float32)
        return 0
    lax.fori_loop(0, accs[0].shape[0] // 128, clear, 0)
    sub = lax.broadcasted_iota(jnp.int32, (8, half), 0)
    diagonal = jnp.where(
        lax.broadcasted_iota(jnp.int32, (16, half), 1) // 16 == (lax.broadcasted_iota(jnp.int32, (16, half), 0) & 7), 1.0, 0.0
    ).astype(jnp.bfloat16)
    k_at = lax.broadcasted_iota(jnp.int32, (width, width), 0)
    n_at = lax.broadcasted_iota(jnp.int32, (width, width), 1)
    repeat = jnp.where((k_at % 16 == n_at % 16) & (k_at // half == n_at // half), 1.0, 0.0).astype(jnp.bfloat16)
    for turn in range(steps):
        table = (near_table, far_table)[turn]

        starts = (chunks + 8 + 8 * turn) * slots
        groups = (list_ref[starts + STARTS * slots] + 2 * EIGHTS - 1) // (2 * EIGHTS)

        def words(g):
            found = []
            for k in range(EIGHTS):
                eight = list_ref.at[pl.ds(list_ref[starts + g * EIGHTS + k], 8)]
                found += [eight[u] for u in range(8)]
            return found

        def load(now, sides, staged=None):
            for side in range(2):
                tiles = []
                for word in now[side * GROUP // 2:(side + 1) * GROUP // 2]:
                    src = word & 8191
                    both = jnp.concatenate(
                        [table[pl.ds(src, 8, stride=0), :], table[pl.ds(src + reps * rows, 8, stride=0), :]], axis=0)
                    tiles.append(both.astype(jnp.bfloat16) * diagonal)
                pairs = [jnp.concatenate(tiles[u:u + 2], axis=1) for u in range(0, GROUP // 2, 2)]
                pltpu.matmul_acc_lhs(sides[side], jnp.concatenate(pairs, axis=0), load_staged_rhs=staged)

        def add_up(now, popped, ring):
            for side in range(2):
                repeated = popped[side]
                for base in range(side * GROUP // 2, (side + 1) * GROUP // 2, 8):
                    lows, highs = [], []
                    for u in range(base, base + 8):
                        maps = bank_ref[pl.ds(pl.multiple_of((now[u] >> 8) & 2016, 32), 32), :]
                        row = u % (GROUP // 2) // 2 * 16
                        lane = u % 2 * half
                        top = repeated[row:row + 8, lane:lane + half]
                        low = repeated[row + 8:row + 16, lane:lane + half]
                        lows.append(maps[0:8] * top + maps[16:24] * low)
                        highs.append(maps[8:16] * top + maps[24:32] * low)
                    for k, parts in enumerate((lows, highs)):
                        message = column_sums([parts[i] for i in (0, 4, 2, 6, 1, 5, 3, 7)], sub)
                        ring[pl.ds(2 * base + k, 8, stride=2), :] = message.astype(jnp.bfloat16).astype(jnp.float32)
            for u in range(GROUP):
                acc = accs[u % ACCS]
                acc[pl.ds(lax.shift_right_logical(now[u], 19), 2), :] += ring[pl.ds(2 * u, 2), :]

        def run(*sides):
            even, odd = sides[:2], sides[2:]
            for side in range(2):
                pltpu.matmul_push_rhs(repeat, 0, side)
            load(words(0), even, 0)
            load(words(1), odd)

            def group(g, carry):
                for which, sides in enumerate((even, odd)):
                    popped = [pltpu.matmul_pop(side) for side in sides]
                    load(words(2 * g + which + 2), sides)
                    add_up(words(2 * g + which), popped, rings[which])
                return carry

            lax.fori_loop(0, groups, group, 0)
            for side in (*even, *odd):
                rings[0][0:8, :] = pltpu.matmul_pop(side)[0:8, 0:half]

        pl.run_scoped(run, *[pltpu.ACC(side)((4 * GROUP, width), jnp.float32) for side in (0, 1, 0, 1)])
    block = 64

    def begin(i, sides):
        halves = []
        for k in range(2):
            where = pl.ds(pl.multiple_of(i * 2 * block, 2 * block) + k, block, stride=2)
            side = accs[0][where, :]
            for a in accs[1:]:
                side = side + a[where, :]
            halves.append(side)
        total = jnp.concatenate(halves, axis=1)
        top = total.astype(jnp.bfloat16)
        low = (total - top.astype(jnp.float32)).astype(jnp.bfloat16)
        pltpu.matmul_acc_lhs(sides[0], top)
        pltpu.matmul_acc_lhs(sides[1], top)
        pltpu.matmul_acc_lhs(sides[0], low)

    def end(i, sides):
        at = pl.ds(pl.multiple_of(i * block, block), block)
        mixed = pltpu.matmul_pop(sides[0]) + pltpu.matmul_pop(sides[1])
        out_ref[at, :] = (own_ref[me, at, :].astype(jnp.float32) + mixed).astype(jnp.bfloat16)

    def mix(*sides):
        lanes = [sides[2 * k:2 * k + 2] for k in range(FLIGHT)]
        blank = jnp.zeros((block, width), jnp.bfloat16)
        for side in range(2):
            pltpu.matmul_push_rhs(spread_ref[side], 0, side)
            pltpu.matmul_acc_lhs(sides[side], blank, load_staged_rhs=0)
        blocks = rows // block
        for k in range(FLIGHT):
            begin(k, lanes[k])

        def some(i, carry):
            for k in range(FLIGHT):
                end(i * FLIGHT + k, lanes[k])
                begin((i + 1) * FLIGHT + k, lanes[k])
            return carry

        lax.fori_loop(0, blocks // FLIGHT - 1, some, 0)
        for k in range(FLIGHT):
            end(blocks - FLIGHT + k, lanes[k])

    pl.run_scoped(mix, *[pltpu.ACC(side)((block, width), jnp.float32) for side in (0, 1) * FLIGHT])


def edges(own, near, far, lists, bank, spread):
    reps, rows, width = own.shape
    chunks = lists.shape[0] // SLOTS - 24
    dims = (reps, rows, width, 2, chunks, SLOTS)
    smem = pl.BlockSpec(memory_space=pltpu.SMEM)
    vmem = pl.BlockSpec(memory_space=pltpu.VMEM)
    return pl.pallas_call(
        functools.partial(edge_kernel, dims),
        out_shape=jax.ShapeDtypeStruct((rows, width), own.dtype),
        in_specs=[vmem, vmem, vmem, smem, vmem, vmem],
        out_specs=vmem,
        scratch_shapes=[
            pltpu.VMEM((2 * GROUP, width // 2), jnp.float32),
            pltpu.VMEM((2 * GROUP, width // 2), jnp.float32),
            *[pltpu.VMEM((2 * rows + 128, width // 2), jnp.float32)] * ACCS,
        ],
        compiler_params=pltpu.CompilerParams(vmem_limit_bytes=16 << 20),
        name="edges",
    )(own, near, far, lists, bank, spread)


def body(features, restriction, mixing, source_index, target_index, map_index, edge_counts):
    rows = features.shape[0]
    stalk = restriction.shape[1]
    channels = mixing.shape[0]
    dims = (lax.axis_size("rep"), lax.axis_size("blk"), rows, stalk, channels)
    own, _, near, far, lists, bank, spread = exchange(
        dims, features, source_index, target_index, map_index, edge_counts, restriction, mixing)
    return edges(own, near, far, lists.reshape(-1), bank, spread)


def solution(mesh):
    in_specs = (
        P(("blk", "rep"), None),
        P(),
        P(),
        P("blk", "rep", None, None),
        P("blk", "rep", None, None),
        P("blk", "rep", None, None),
        P("blk", "rep", None),
    )
    out_specs = P(("blk", "rep"), None)
    step = jax.shard_map(body, mesh=mesh, in_specs=in_specs, out_specs=out_specs, check_vma=False)

    def run(*args):
        with jax.sharding.use_abstract_mesh(mesh.abstract_mesh):
            return step(*args)

    return run
```

```python
import functools

import jax
import jax.numpy as jnp
from jax import lax
from jax.experimental import pallas as pl
from jax.experimental.pallas import tpu as pltpu
from jax.sharding import PartitionSpec as P

MESH = pl.DeviceIdType.MESH
PIECES = 4
SLOTS = 256
BLOCK = 8192
STARTS = 5
GROUP = 48
EIGHTS = GROUP // 8
ACCS = 4
FLIGHT = 4


def exchange_kernel(dims, features, source_ref, target_ref, map_ref, count_ref, restriction_ref, mixing_ref,
                    own, prev, near_table, far_table, list_ref, bank_ref, spread_ref,
                    sources, targets, maps, counts, restrictions, mixings, packed, position,
                    home_sem, index_send, index_recv, send, recv):
    reps, blocks, rows, stalk, channels = dims
    width = stalk * channels
    half = width // 2
    rep = lax.axis_index("rep")
    blk = lax.axis_index("blk")
    pair = lax.rem(rep + 2, 4)
    mate = rep + 1 - 2 * lax.rem(rep, 2)
    far = lax.rem(mate + 2, 4)
    after = lax.rem(blk + 1, blocks)
    before = lax.rem(blk + blocks - 1, blocks)
    to_mate = {"rep": mate, "blk": blk}
    to_pair = {"rep": pair, "blk": blk}
    to_next = {"rep": pair, "blk": after}
    from_last = {"rep": pair, "blk": before}

    home = [pltpu.make_async_copy(src, dst, home_sem.at[k]) for k, (src, dst) in enumerate((
        (source_ref, sources.at[rep]), (target_ref, targets.at[rep]), (map_ref, maps.at[rep]), (count_ref, counts.at[rep]),
        (features, own.at[rep]), (restriction_ref, restrictions), (mixing_ref, mixings)))]
    for copy in home:
        copy.start()

    barrier = pltpu.get_barrier_semaphore()
    for other in (to_mate, to_pair, to_next, from_last):
        pl.semaphore_signal(barrier, inc=1, device_id=other, device_id_type=MESH)
    pl.semaphore_wait(barrier, 4)

    index_copies = []
    for a, (src, dst) in enumerate(((source_ref, sources), (target_ref, targets), (map_ref, maps), (count_ref, counts))):
        for k, (part, place, other) in enumerate((
                (src, rep, to_mate), (src, rep, to_pair), (dst.at[pair], pair, to_mate))):
            index_copies.append(pltpu.make_async_remote_copy(
                src_ref=part, dst_ref=dst.at[place], send_sem=index_send.at[a, k], recv_sem=index_recv.at[a, k],
                device_id=other, device_id_type=MESH))
    for a in range(4):
        index_copies[3 * a + 1].start()
        index_copies[3 * a].start()

    piece = rows // PIECES

    def rows_of(k):
        return pl.ds(k * piece, piece)

    def remote(family, k, src, dst, other):
        return pltpu.make_async_remote_copy(
            src_ref=src, dst_ref=dst, send_sem=send.at[family, k], recv_sem=recv.at[family, k],
            device_id=other, device_id_type=MESH)

    every = range(PIECES)
    first, second = range(PIECES // 2), range(PIECES // 2, PIECES)
    to_mate_own = [remote(0, k, features.at[rows_of(k), :], own.at[rep, rows_of(k), :], to_mate) for k in every]
    to_pair_own = [remote(1, k, features.at[rows_of(k), :], own.at[rep, rows_of(k), :], to_pair) for k in every]
    to_next_own = [remote(2, k, features.at[rows_of(k), :], prev.at[rep, rows_of(k), :], to_next) for k in every]
    mate_pairs = [remote(3, k, own.at[pair, rows_of(k), :], own.at[pair, rows_of(k), :], to_mate) for k in every]
    mate_lasts = [remote(4, k, prev.at[pair, rows_of(k), :], prev.at[pair, rows_of(k), :], to_mate) for k in every]
    next_pairs = [remote(5, k, own.at[pair, rows_of(k), :], prev.at[pair, rows_of(k), :], to_next) for k in first]
    pair_lasts = [remote(6, k - PIECES // 2, prev.at[pair, rows_of(k), :], prev.at[pair, rows_of(k), :], to_pair) for k in second]
    mate_rest = [remote(7, k, prev.at[rep, rows_of(k), :], prev.at[rep, rows_of(k), :], to_mate) for k in every]

    for k in every:
        to_next_own[k].start()
        to_pair_own[k].start()
    for k in every:
        to_mate_own[k].start()

    for copy in home:
        copy.wait()
    for a in range(4):
        index_copies[3 * a + 1].wait_recv()
        index_copies[3 * a + 2].start()
    for a in range(4):
        index_copies[3 * a].wait_recv()
        index_copies[3 * a + 2].wait_recv()
    steps, capacity = source_ref.shape[2:]
    runs = capacity // SLOTS
    chunks = reps * runs * steps
    spot = lax.broadcasted_iota(jnp.int32, (steps, SLOTS), 1)
    for r in range(reps):
        live = counts[r, 0]
        live = jnp.concatenate([jnp.broadcast_to(live[:, s:s + 1], (1, SLOTS)) for s in range(steps)], axis=0)
        for j in range(runs):
            part = pl.ds(j * SLOTS, SLOTS)
            to = sources.at[r, 0, 0, :, part][...]
            hit = targets.at[r, 0, 0, :, part][...]
            by = maps.at[r, 0, 0, :, part][...]
            here = (hit // rows == rep) & (spot + j * SLOTS < live)
            at = pl.ds((r * runs + j) * steps, steps)
            packed[at, :] = to + by * BLOCK + (hit & (rows - 1)) * (BLOCK * 128)
            position[at, :] = jnp.where(here, 1, 0)
    earlier = (lax.broadcasted_iota(jnp.int32, (SLOTS, SLOTS), 0) <= lax.broadcasted_iota(jnp.int32, (SLOTS, SLOTS), 1))
    here = position[...]
    running = jnp.dot(
        here.astype(jnp.float32).astype(jnp.bfloat16), earlier.astype(jnp.float32).astype(jnp.bfloat16),
        preferred_element_type=jnp.float32).astype(jnp.int32)
    eights = (running[:, SLOTS - 1:SLOTS] + 7) // 8
    chunk_of = lax.broadcasted_iota(jnp.int32, (chunks, 1), 0)
    ahead = jnp.where(
        lax.broadcasted_iota(jnp.int32, (chunks, chunks), 1) < lax.broadcasted_iota(jnp.int32, (chunks, chunks), 0), 1.0, 0.0)
    run = lax.broadcasted_iota(jnp.int32, (chunks, STARTS * SLOTS), 1)
    for t in range(steps):
        mine = jnp.where(chunk_of % steps == t, eights, 0)
        mine_wide = jnp.broadcast_to(mine, (chunks, SLOTS))
        begun = jnp.dot(
            ahead.astype(jnp.bfloat16), mine_wide.astype(jnp.float32).astype(jnp.bfloat16),
            preferred_element_type=jnp.float32).astype(jnp.int32)[:, 0:1]
        inside = (run >= begun) & (run < begun + mine)
        table_row = jnp.sum(
            jnp.where(inside, (chunk_of - chunks) * SLOTS + 8 * (run - begun), 0), axis=0, keepdims=True) + chunks * SLOTS
        to = chunks + 8 + 8 * t
        for k in range(STARTS):
            list_ref[to + k:to + k + 1, :] = table_row[:, k * SLOTS:(k + 1) * SLOTS]
        list_ref[to + STARTS:to + STARTS + 1, :] = jnp.sum(mine_wide, axis=0, keepdims=True)
    position[...] = jnp.where(here > 0, running - 1, -1)
    unused = rows * (BLOCK * 128) - 2**32
    shift = 8 * jnp.minimum(lax.broadcasted_iota(jnp.int32, (8, SLOTS), 0), 3)
    used = lax.broadcasted_iota(jnp.int32, (8, SLOTS), 0) < 4
    place = lax.broadcasted_iota(jnp.int32, (SLOTS, SLOTS), 0)
    slot = lax.broadcasted_iota(jnp.int32, (8, SLOTS), 1)
    list_ref[chunks:chunks + 8, :] = jnp.full((8, SLOTS), unused, jnp.int32)

    def compress(c, carry):
        at = position[pl.ds(c, 1), :]
        word = jnp.broadcast_to(packed[pl.ds(c, 1), :], (8, SLOTS))
        digits = (lax.shift_right_logical(word, shift) & 255).astype(jnp.float32).astype(jnp.bfloat16)
        chosen = jnp.where(place == at, 1.0, 0.0).astype(jnp.bfloat16)
        moved = lax.dot_general(digits, chosen, (((1,), (1,)), ((), ())), preferred_element_type=jnp.float32)
        whole = jnp.where(used, moved.astype(jnp.int32) << shift, 0)
        whole = jnp.sum(whole, axis=0, keepdims=True)
        total = jnp.max(jnp.broadcast_to(at, (8, SLOTS)), axis=1, keepdims=True) + 1
        list_ref[pl.ds(c, 1), :] = jnp.where(slot < total, jnp.broadcast_to(whole, (8, SLOTS)), unused)[0:1]
        return carry

    lax.fori_loop(0, chunks, compress, 0)

    def three(x):
        high = x.astype(jnp.bfloat16)
        left = x - high.astype(jnp.float32)
        middle = left.astype(jnp.bfloat16)
        return high, middle, (left - middle.astype(jnp.float32)).astype(jnp.bfloat16)

    def ones(shape, test):
        return jnp.where(
            test(lax.broadcasted_iota(jnp.int32, shape, 0), lax.broadcasted_iota(jnp.int32, shape, 1)), 1.0, 0.0
        ).astype(jnp.bfloat16)

    count = restrictions.shape[2]
    wide = ones((stalk, width), lambda p, q: p == q // channels)
    for j in range(stalk):
        total = jnp.zeros((count, width), jnp.float32)
        for part in three(restrictions[:, j, :]):
            total = total + lax.dot_general(part, wide, (((0,), (0,)), ((), ())), preferred_element_type=jnp.float32)
        for l in range(2):
            bank_ref[pl.ds(j // 8 * 16 + l * 8 + j % 8, count, stride=2 * stalk), :] = total[:, l * half:(l + 1) * half]

    tall = ones((width, channels), lambda p, q: (p & (channels - 1)) == q)
    broad = ones((channels, width), lambda p, q: p == (q & (channels - 1)))
    blocked = ones((width, width), lambda p, q: p // channels == q // channels)
    for k, part in enumerate(three(mixings[...])[:2]):
        part = jnp.dot(tall, part, preferred_element_type=jnp.float32).astype(jnp.bfloat16)
        spread_ref[k] = jnp.dot(part, broad, preferred_element_type=jnp.float32).astype(jnp.bfloat16) * blocked

    def widen(block, table, shard, k):
        def some(i, carry):
            at = pl.multiple_of(k * piece + i * 128, 128)
            rows_in = block[shard, pl.ds(at, 128), :].astype(jnp.float32)
            table[pl.ds(pl.multiple_of(shard * rows + at, 128), 128), :] = rows_in[:, 0:half]
            table[pl.ds(pl.multiple_of((reps + shard) * rows + at, 128), 128), :] = rows_in[:, half:width]
            return carry

        lax.fori_loop(0, piece // 128, some, 0)

    for k in every:
        to_mate_own[k].wait_recv()
        widen(own, near_table, rep, k)
        widen(own, near_table, mate, k)
    for k in every:
        to_pair_own[k].wait_recv()
        if k in first:
            next_pairs[k].start()
        to_next_own[k].wait_recv()
        if k in second:
            pair_lasts[k - PIECES // 2].start()
        mate_pairs[k].start()
        mate_lasts[k].start()
        widen(own, near_table, pair, k)
        widen(prev, far_table, pair, k)
        if k > 0:
            mate_pairs[k - 1].wait_recv()
            mate_lasts[k - 1].wait_recv()
            widen(own, near_table, far, k - 1)
            widen(prev, far_table, far, k - 1)
    for k in first:
        next_pairs[k].wait_recv()
        mate_rest[k].start()
        pair_lasts[k].wait_recv()
        mate_rest[k + PIECES // 2].start()
        if k == 0:
            mate_pairs[PIECES - 1].wait_recv()
            mate_lasts[PIECES - 1].wait_recv()
            widen(own, near_table, far, PIECES - 1)
            widen(prev, far_table, far, PIECES - 1)
        else:
            for j in (k - 1, k - 1 + PIECES // 2):
                mate_rest[j].wait_recv()
                widen(prev, far_table, mate, j)
        widen(prev, far_table, rep, k)
        widen(prev, far_table, rep, k + PIECES // 2)
    for j in (PIECES // 2 - 1, PIECES - 1):
        mate_rest[j].wait_recv()
        widen(prev, far_table, mate, j)
    for copy in index_copies:
        copy.wait_send()
    for family in (to_mate_own, to_pair_own, to_next_own, mate_pairs, mate_lasts, next_pairs, pair_lasts, mate_rest):
        for copy in family:
            copy.wait_send()


def exchange(dims, features, sources, targets, maps, counts, restriction, mixing):
    reps, blocks, rows, stalk, channels = dims
    width = stalk * channels
    chunks = reps * sources.size // SLOTS
    restriction = jnp.transpose(restriction, (1, 2, 0))
    operands = [pltpu.with_memory_space_constraint(x, pltpu.HBM) for x in (
        features, sources, targets, maps, counts, restriction, mixing)]
    vmem = pl.BlockSpec(memory_space=pltpu.VMEM)
    return pl.pallas_call(
        functools.partial(exchange_kernel, dims),
        out_shape=(
            pltpu.VMEM((reps, rows, width), features.dtype),
            pltpu.VMEM((reps, rows, width), features.dtype),
            pltpu.VMEM((2 * reps * rows, width // 2), jnp.float32),
            pltpu.VMEM((2 * reps * rows, width // 2), jnp.float32),
            pltpu.VMEM((chunks + 24, SLOTS), jnp.int32),
            pltpu.VMEM((2 * restriction.shape[2] * stalk, width // 2), jnp.float32),
            pltpu.VMEM((2, width, width), jnp.bfloat16),
        ),
        in_specs=[pl.BlockSpec(memory_space=pltpu.HBM)] * 7,
        out_specs=(vmem,) * 7,
        scratch_shapes=[
            pltpu.VMEM((reps, *sources.shape), jnp.int32),
            pltpu.VMEM((reps, *sources.shape), jnp.int32),
            pltpu.VMEM((reps, *sources.shape), jnp.int32),
            pltpu.VMEM((reps, *counts.shape), jnp.int32),
            pltpu.VMEM(restriction.shape, restriction.dtype),
            pltpu.VMEM(mixing.shape, mixing.dtype),
            pltpu.VMEM((chunks, SLOTS), jnp.int32),
            pltpu.VMEM((chunks, SLOTS), jnp.int32),
            pltpu.SemaphoreType.DMA((7,)),
            pltpu.SemaphoreType.DMA((4, 3)),
            pltpu.SemaphoreType.DMA((4, 3)),
            pltpu.SemaphoreType.DMA((8, PIECES)),
            pltpu.SemaphoreType.DMA((8, PIECES)),
        ],
        compiler_params=pltpu.CompilerParams(collective_id=0, has_side_effects=True, vmem_limit_bytes=8 << 20),
        name="exchange",
    )(*operands)


def column_sums(parts, sub):
    step = 1
    while len(parts) > 1:
        keep = (sub & step) == 0
        half = len(parts) // 2
        joined = []
        for a, b in zip(parts[:half], parts[half:]):
            joined.append(jnp.where(keep, a, b) + pltpu.roll(jnp.where(keep, b, a), step, 0))
        parts = joined
        step *= 2
    return parts[0]


def edge_kernel(dims, own_ref, near_table, far_table, list_ref, bank_ref, spread_ref, out_ref,
                ring_even, ring_odd, *rest):
    reps, rows, width, steps, chunks, slots = dims
    accs = rest
    half = width // 2
    rings = (ring_even, ring_odd)
    me = lax.axis_index("rep")
    def clear(i, _):
        at = pl.ds(pl.multiple_of(i * 128, 128), 128)
        for a in accs:
            a[at, :] = jnp.zeros((128, half), jnp.float32)
        return 0
    lax.fori_loop(0, accs[0].shape[0] // 128, clear, 0)
    sub = lax.broadcasted_iota(jnp.int32, (8, half), 0)
    diagonal = jnp.where(
        lax.broadcasted_iota(jnp.int32, (16, half), 1) // 16 == (lax.broadcasted_iota(jnp.int32, (16, half), 0) & 7), 1.0, 0.0
    ).astype(jnp.bfloat16)
    k_at = lax.broadcasted_iota(jnp.int32, (width, width), 0)
    n_at = lax.broadcasted_iota(jnp.int32, (width, width), 1)
    repeat = jnp.where((k_at % 16 == n_at % 16) & (k_at // half == n_at // half), 1.0, 0.0).astype(jnp.bfloat16)
    for turn in range(steps):
        table = (near_table, far_table)[turn]

        starts = (chunks + 8 + 8 * turn) * slots
        groups = (list_ref[starts + STARTS * slots] + 2 * EIGHTS - 1) // (2 * EIGHTS)

        def words(g):
            found = []
            for k in range(EIGHTS):
                eight = list_ref.at[pl.ds(list_ref[starts + g * EIGHTS + k], 8)]
                found += [eight[u] for u in range(8)]
            return found

        def load(now, sides, staged=None):
            for side in range(2):
                tiles = []
                for word in now[side * GROUP // 2:(side + 1) * GROUP // 2]:
                    src = word & 8191
                    both = jnp.concatenate(
                        [table[pl.ds(src, 8, stride=0), :], table[pl.ds(src + reps * rows, 8, stride=0), :]], axis=0)
                    tiles.append(both.astype(jnp.bfloat16) * diagonal)
                pairs = [jnp.concatenate(tiles[u:u + 2], axis=1) for u in range(0, GROUP // 2, 2)]
                pltpu.matmul_acc_lhs(sides[side], jnp.concatenate(pairs, axis=0), load_staged_rhs=staged)

        def add_up(now, popped, ring):
            for side in range(2):
                repeated = popped[side]
                for base in range(side * GROUP // 2, (side + 1) * GROUP // 2, 8):
                    lows, highs = [], []
                    for u in range(base, base + 8):
                        maps = bank_ref[pl.ds(pl.multiple_of((now[u] >> 8) & 2016, 32), 32), :]
                        row = u % (GROUP // 2) // 2 * 16
                        lane = u % 2 * half
                        top = repeated[row:row + 8, lane:lane + half]
                        low = repeated[row + 8:row + 16, lane:lane + half]
                        lows.append(maps[0:8] * top + maps[16:24] * low)
                        highs.append(maps[8:16] * top + maps[24:32] * low)
                    for k, parts in enumerate((lows, highs)):
                        message = column_sums([parts[i] for i in (0, 4, 2, 6, 1, 5, 3, 7)], sub)
                        ring[pl.ds(2 * base + k, 8, stride=2), :] = message.astype(jnp.bfloat16).astype(jnp.float32)
            for u in range(GROUP):
                acc = accs[u % ACCS]
                acc[pl.ds(lax.shift_right_logical(now[u], 19), 2), :] += ring[pl.ds(2 * u, 2), :]

        def run(*sides):
            even, odd = sides[:2], sides[2:]
            for side in range(2):
                pltpu.matmul_push_rhs(repeat, 0, side)
            load(words(0), even, 0)
            load(words(1), odd)

            def group(g, carry):
                for which, sides in enumerate((even, odd)):
                    popped = [pltpu.matmul_pop(side) for side in sides]
                    load(words(2 * g + which + 2), sides)
                    add_up(words(2 * g + which), popped, rings[which])
                return carry

            lax.fori_loop(0, groups, group, 0)
            for side in (*even, *odd):
                rings[0][0:8, :] = pltpu.matmul_pop(side)[0:8, 0:half]

        pl.run_scoped(run, *[pltpu.ACC(side)((4 * GROUP, width), jnp.float32) for side in (0, 1, 0, 1)])
    block = 64

    def begin(i, sides):
        halves = []
        for k in range(2):
            where = pl.ds(pl.multiple_of(i * 2 * block, 2 * block) + k, block, stride=2)
            side = accs[0][where, :]
            for a in accs[1:]:
                side = side + a[where, :]
            halves.append(side)
        total = jnp.concatenate(halves, axis=1)
        top = total.astype(jnp.bfloat16)
        low = (total - top.astype(jnp.float32)).astype(jnp.bfloat16)
        pltpu.matmul_acc_lhs(sides[0], top)
        pltpu.matmul_acc_lhs(sides[1], top)
        pltpu.matmul_acc_lhs(sides[0], low)

    def end(i, sides):
        at = pl.ds(pl.multiple_of(i * block, block), block)
        mixed = pltpu.matmul_pop(sides[0]) + pltpu.matmul_pop(sides[1])
        out_ref[at, :] = (own_ref[me, at, :].astype(jnp.float32) + mixed).astype(jnp.bfloat16)

    def mix(*sides):
        lanes = [sides[2 * k:2 * k + 2] for k in range(FLIGHT)]
        blank = jnp.zeros((block, width), jnp.bfloat16)
        for side in range(2):
            pltpu.matmul_push_rhs(spread_ref[side], 0, side)
            pltpu.matmul_acc_lhs(sides[side], blank, load_staged_rhs=0)
        blocks = rows // block
        for k in range(FLIGHT):
            begin(k, lanes[k])

        def some(i, carry):
            for k in range(FLIGHT):
                end(i * FLIGHT + k, lanes[k])
                begin((i + 1) * FLIGHT + k, lanes[k])
            return carry

        lax.fori_loop(0, blocks // FLIGHT - 1, some, 0)
        for k in range(FLIGHT):
            end(blocks - FLIGHT + k, lanes[k])

    pl.run_scoped(mix, *[pltpu.ACC(side)((block, width), jnp.float32) for side in (0, 1) * FLIGHT])


def edges(own, near, far, lists, bank, spread):
    reps, rows, width = own.shape
    chunks = lists.shape[0] // SLOTS - 24
    dims = (reps, rows, width, 2, chunks, SLOTS)
    smem = pl.BlockSpec(memory_space=pltpu.SMEM)
    vmem = pl.BlockSpec(memory_space=pltpu.VMEM)
    return pl.pallas_call(
        functools.partial(edge_kernel, dims),
        out_shape=jax.ShapeDtypeStruct((rows, width), own.dtype),
        in_specs=[vmem, vmem, vmem, smem, vmem, vmem],
        out_specs=vmem,
        scratch_shapes=[
            pltpu.VMEM((2 * GROUP, width // 2), jnp.float32),
            pltpu.VMEM((2 * GROUP, width // 2), jnp.float32),
            *[pltpu.VMEM((2 * rows + 128, width // 2), jnp.float32)] * ACCS,
        ],
        compiler_params=pltpu.CompilerParams(vmem_limit_bytes=16 << 20),
        name="edges",
    )(own, near, far, lists, bank, spread)


def body(features, restriction, mixing, source_index, target_index, map_index, edge_counts):
    rows = features.shape[0]
    stalk = restriction.shape[1]
    channels = mixing.shape[0]
    dims = (lax.axis_size("rep"), lax.axis_size("blk"), rows, stalk, channels)
    own, _, near, far, lists, bank, spread = exchange(
        dims, features, source_index, target_index, map_index, edge_counts, restriction, mixing)
    return edges(own, near, far, lists.reshape(-1), bank, spread)


def solution(mesh):
    in_specs = (
        P(("blk", "rep"), None),
        P(),
        P(),
        P("blk", "rep", None, None),
        P("blk", "rep", None, None),
        P("blk", "rep", None, None),
        P("blk", "rep", None),
    )
    out_specs = P(("blk", "rep"), None)
    step = jax.shard_map(body, mesh=mesh, in_specs=in_specs, out_specs=out_specs, check_vma=False)

    def run(*args):
        with jax.sharding.use_abstract_mesh(mesh.abstract_mesh):
            return step(*args)

    return run
```
